32 devices in a mesh: tm: 8 (over z, y), scene: 4 (over x, core).
Axes of the slice: x: 2, y: 2, z: 4, core: 2. Of those that a mesh axis runs over, the one named last changes fastest.
Arguments:
- frames: bfloat16 [512, 2, 32, 384], P('tm', None, 'scene'), may hold values from -6 to 6
- conv_weight: bfloat16 [3, 3, 3, 384, 384], replicated, may hold values from -0.0625 to 0.0625
- down_weight: bfloat16 [8, 384, 384], replicated, may hold values from -0.109375 to 0.109375
- w_query: bfloat16 [384, 384], replicated, may hold values from -64 to 64
- w_key: bfloat16 [384, 384], replicated, may hold values from -2 to 2
- w_value: bfloat16 [384, 384], replicated, may hold values from -0.3125 to 0.3125
- w_out: bfloat16 [384, 384], replicated, may hold values from -0.3125 to 0.3125
- shot_lengths: int32 [4], replicated, may hold values from 1 to 32, 64 in all
- scene_label: int32 [64, 1], P('tm'), may hold values from 0 to 3; in each aligned block of 8 rows (0 to 7, 8 to 15, ...) at most 4 rows name the same one
- out_grad: bfloat16 [512, 2, 32, 384], P('tm', None, 'scene'), may hold values from -6 to 6
Outputs:
- latent_out: bfloat16 [64, 2, 32, 384], P('tm', None, 'scene')
- frame_grad: bfloat16 [512, 2, 32, 384], P('tm', None, 'scene')
The draws below stay inside these ranges and needn't reach their ends.
Inputs may be any that keep to these rules, and one draw needn't show every extreme that they name: `shot_lengths`: the lengths sum to 64; the longest is exactly 32. `scene_label`: within each aligned block of 8 latent frames (those of one index of tm) no label occurs more than 4 times; in some block one label occurs exactly 4 times.
All inputs are finite; a program needn't handle non-finite values.
Results may differ from the reference program's by a relative error of at most 0.008.
Values may be sent and summed in bfloat16 or wider, within the bound.
A program may use at most 128 MiB of HBM per device.

```python
import math
import jax
import jax.numpy as jnp
import numpy as np
from jax import lax

C = 384
HEAD = 64
H = 2
SHOTS = 4
LF = 8
LAT = 64
FRAMES = 512
W = 32
MOST = 32
CAP = 4
N_SCENE = 4


def shared_base(key):
    raw = jax.random.normal(jax.random.fold_in(key, 7), (C, C), jnp.float32)
    return jnp.clip(raw, -6.0, 6.0) / math.sqrt(C)


def draw_w_key(key, part):
    return shared_base(key).astype(jnp.bfloat16)


def draw_w_query(key, part):
    raw = jax.random.normal(jax.random.fold_in(key, 9), (C, C), jnp.float32)
    own = jnp.clip(raw, -6.0, 6.0) / math.sqrt(C)
    return own.astype(jnp.bfloat16)


def levels(stream_key, extent, split, low, largest):
    def one(position, shards_of):
        steps = jax.random.uniform(jax.random.fold_in(jax.random.fold_in(stream_key, 6), position), (shards_of,), jnp.float32, low / len(split), largest / len(split))
        return jnp.repeat(jnp.exp(steps), extent[position] // shards_of).reshape((-1,) + (1,) * (len(extent) - position - 1))

    loudness = one(*split[0])
    for cut in split[1:]:
        loudness = loudness * one(*cut)
    return loudness


def length_profile(count, total, bound, lean):
    portions = [(1 << 20) // math.isqrt(standing ** lean) + 1 for standing in range(2, count + 1)]
    surplus, holding = total - bound - (count - 1), [1] * (count - 1)
    while surplus > 0:
        free = [i for i in range(count - 1) if holding[i] < bound]
        whole, remaining = sum([portions[i] for i in free]), surplus
        for i in free:
            extra = min(bound - holding[i], max(1, remaining * portions[i] // whole), surplus)
            holding[i] = holding[i] + extra
            surplus = surplus - extra
    return np.array([bound] + holding)


def ragged_sizes(key, amount, total, limit, lean):
    if amount == 2:
        one = jax.random.randint(key, (), max(1, total - limit), min(limit, total - 1) + 1)
        return jnp.stack([one, total - one])
    sizes = jnp.asarray(length_profile(amount, total, limit, lean), jnp.int32)
    pairs = (amount - 1) // 2
    donor, receiver = sizes[1:1 + 2 * pairs:2], sizes[2:2 + 2 * pairs:2]
    margin = jnp.minimum(donor - 1, limit - receiver)
    moved = jax.random.randint(jax.random.fold_in(key, 1), (pairs,), 0, 1 << 20) % (margin + 1)
    sizes = sizes.at[1:1 + 2 * pairs:2].set(donor - moved).at[2:2 + 2 * pairs:2].set(receiver + moved)
    return sizes[jax.random.permutation(jax.random.fold_in(key, 2), amount)]


def assign_block(rng, own, number, rows, number_of, top, bound, slope):
    ranking = jax.random.permutation(rng, number_of)
    crowded, common = load_shares(number_of, rows * top, bound, slope, True), load_shares(number_of, rows * top, bound, slope, False)
    places = jnp.arange(number_of)

    def named(tallies, offset_by):
        used = int((tallies > 0).sum())
        fixed = max(1, used // 4)
        moved = fixed + (places - fixed + offset_by * (used - fixed)) % max(1, number_of - fixed)
        return jnp.zeros((number_of,), jnp.int32).at[ranking[jnp.where(places < fixed, places, moved)]].set(jnp.asarray(tallies, jnp.int32))

    tallies = jnp.where(number % 4 == 0, named(crowded, number // 4), named(common, number - number // 4 - 1))
    mixed = jax.random.permutation(jax.random.fold_in(own, 3), number_of)
    donor, receiver = mixed[0:number_of // 2 * 2:2], mixed[1:number_of // 2 * 2:2]
    slack = jnp.minimum(tallies[donor] - 1, bound - tallies[receiver]) // 2
    slack = jnp.where((donor == ranking[0]) | (receiver == ranking[0]) | (tallies[receiver] == 0), 0, jnp.maximum(slack, 0))
    moved = jax.random.randint(jax.random.fold_in(own, 4), (number_of // 2,), 0, 1 << 20) % (slack + 1)
    tallies = tallies.at[donor].add(-moved).at[receiver].add(moved)
    items = jnp.searchsorted(jnp.cumsum(tallies), jnp.arange(rows * top), side="right").astype(jnp.int32)
    listing = items.reshape(top, rows).T
    listing = listing[jax.random.permutation(jax.random.fold_in(own, 1), rows)]
    offset_by = jax.random.randint(jax.random.fold_in(own, 2), (rows, 1), 0, top)
    return jnp.take_along_axis(listing, (jnp.arange(top)[None, :] + offset_by) % top, axis=1)


def load_shares(count, total, limit, skew, full):
    weights = [(1 << 20) // math.isqrt(standing ** skew) + 1 for standing in range(1, count + 1)]
    largest = limit if full else min(limit, max(-(-total // count), total * weights[0] // sum(weights)))
    least = 1 if total - largest >= count - 1 else 0
    given, spare = [largest] + [least] * (count - 1), total - largest - least * (count - 1)
    while spare > 0:
        free = [i for i in range(1, count) if given[i] < largest] or [i for i in range(1, count) if given[i] < limit]
        pool, budget = sum([weights[i] for i in free]), spare
        for i in free:
            addition = min(limit - given[i], max(1, budget * weights[i] // pool), spare)
            given[i] = given[i] + addition
            spare = spare - addition
    return np.array(given)


def bell_draw(stream_key, extent, width, most, shards=(), kind=jnp.bfloat16):
    entries = width * jax.random.normal(stream_key, extent, jnp.float32)
    if shards:
        entries = entries * levels(stream_key, extent, shards, -0.22, 0.18)
    return jnp.clip(entries, -most, most).astype(kind)


def setup_inputs(seed: int = 0) -> dict:
    key_of = jax.random.split(jax.random.key(seed), 11)
    frames = bell_draw(key_of[0], (FRAMES, H, W, C), 1.0, 6.0, ((0, 8), (2, 4)))
    conv_weight = bell_draw(key_of[1], (3, 3, 3, C, C), (27 * C) ** -0.5, 0.0625)
    down_weight = bell_draw(key_of[2], (8, C, C), (8 * C) ** -0.5, 0.109375)
    w_query = draw_w_query(jax.random.fold_in(key_of[10], 71), 0)
    w_key = draw_w_key(jax.random.fold_in(key_of[10], 71), 0)
    w_value = bell_draw(key_of[5], (C, C), C ** -0.5, 0.3125)
    w_out = bell_draw(key_of[6], (C, C), C ** -0.5, 0.3125)
    shot_lengths = ragged_sizes(key_of[7], SHOTS, LAT, MOST, 2).astype(jnp.int32)
    scene_label_keys = jax.random.split(jax.random.fold_in(key_of[8], 1), LAT // LF)
    scene_label_turns = jax.random.permutation(jax.random.fold_in(key_of[8], 3), LAT // LF)
    scene_label = jax.vmap(lambda own, number: assign_block(jax.random.fold_in(key_of[8], 2), own, number, LF, N_SCENE, 1, CAP, 2))(scene_label_keys, scene_label_turns).reshape((LAT, 1))
    out_grad = bell_draw(key_of[9], (FRAMES, H, W, C), 1.0, 6.0, ((0, 8), (2, 4)))
    return dict(frames=frames, conv_weight=conv_weight, down_weight=down_weight, w_query=w_query, w_key=w_key, w_value=w_value, w_out=w_out, shot_lengths=shot_lengths, scene_label=scene_label, out_grad=out_grad)


def conv_block(padded, weight):
    frame_count = padded.shape[0] - 2
    row_count = padded.shape[1] - 2
    col_count = padded.shape[2] - 2
    chans = padded.shape[3]
    total = jnp.zeros((frame_count * row_count * col_count, weight.shape[4]), jnp.float32)
    for shift_t in range(3):
        for shift_h in range(3):
            pieces = [padded[shift_t:shift_t + frame_count, shift_h:shift_h + row_count, shift_w:shift_w + col_count] for shift_w in range(3)]
            stacked = jnp.concatenate(pieces, axis=-1).reshape(-1, 3 * chans)
            total = total + jnp.dot(stacked, weight[shift_t, shift_h].reshape(3 * chans, -1), preferred_element_type=jnp.float32)
    return total.reshape(frame_count, row_count, col_count, -1)

def slope_of(pre):
    gate_value = jax.nn.sigmoid(pre)
    return gate_value * (1.0 + pre * (1.0 - gate_value))

def attend_ref(query_tok, key_tok, allowed, w_query, w_key, w_value, w_out):
    head_count = query_tok.shape[1] // HEAD
    query_proj = jnp.dot(query_tok, w_query, preferred_element_type=jnp.float32).astype(jnp.bfloat16).reshape(-1, head_count, HEAD)
    key_proj = jnp.dot(key_tok, w_key, preferred_element_type=jnp.float32).astype(jnp.bfloat16).reshape(-1, head_count, HEAD)
    value_proj = jnp.dot(key_tok, w_value, preferred_element_type=jnp.float32).astype(jnp.bfloat16).reshape(-1, head_count, HEAD)
    scores = jnp.einsum('qhd,khd->hqk', query_proj.astype(jnp.float32), key_proj.astype(jnp.float32)) * (1.0 / math.sqrt(HEAD))
    scores = jnp.where(allowed[None], scores, -1000000000.0)
    top = lax.optimization_barrier(jnp.max(scores, axis=-1, keepdims=True))
    expo = jnp.exp(scores - top)
    probs = (expo / lax.optimization_barrier(jnp.sum(expo, axis=-1, keepdims=True))).astype(jnp.bfloat16)
    heads_out = jnp.einsum('hqk,khd->qhd', probs.astype(jnp.float32), value_proj.astype(jnp.float32)).astype(jnp.bfloat16)
    heads_out = heads_out.reshape(-1, head_count * HEAD)
    return (query_tok.astype(jnp.float32) + jnp.dot(heads_out, w_out, preferred_element_type=jnp.float32)).astype(jnp.bfloat16)

def reference(frames, conv_weight, down_weight, w_query, w_key, w_value, w_out, shot_lengths, scene_label, out_grad):
    padded = jnp.pad(frames, ((2, 0), (1, 1), (1, 1), (0, 0)))
    pre = conv_block(padded, conv_weight)
    act = (frames.astype(jnp.float32) + jax.nn.silu(pre)).astype(jnp.bfloat16)
    grouped = act.reshape(LAT, 8, H, W, C)
    latent = jnp.einsum('jkhwc,kcd->jhwd', grouped.astype(jnp.float32), down_weight.astype(jnp.float32)).astype(jnp.bfloat16)
    starts = (jnp.cumsum(shot_lengths) - shot_lengths).astype(jnp.int32)
    times = jnp.arange(LAT, dtype=jnp.int32)
    is_start = jnp.any(starts[None, :] == times[:, None], axis=1)
    begin = lax.optimization_barrier(jnp.max(jnp.where(starts[None, :] <= times[:, None], starts[None, :], 0), axis=1)).astype(jnp.int32)
    counts = (times - begin + 1).astype(jnp.float32)

    def advance(carry, inputs):
        frame_lat, flag = inputs
        fresh = jnp.where(flag, frame_lat.astype(jnp.float32), carry + frame_lat.astype(jnp.float32))
        return (fresh, fresh)
    _, shot_sum = lax.scan(advance, jnp.zeros((H, W, C), jnp.float32), (latent, is_start))
    mixed = (latent.astype(jnp.float32) + shot_sum / counts[:, None, None, None]).astype(jnp.bfloat16)
    block_count = LAT // LF
    tokens = mixed.reshape(block_count, LF * H * W, C)
    labels = scene_label[:, 0].reshape(block_count, LF)
    order = jnp.arange(LF, dtype=jnp.int32)

    def per_block(inputs):
        block_tok, block_lab = inputs
        same_frame = (block_lab[None, :] == block_lab[:, None]) & (order[None, :] <= order[:, None])
        allowed = jnp.repeat(jnp.repeat(same_frame, H * W, axis=0), H * W, axis=1)
        return attend_ref(block_tok, block_tok, allowed, w_query, w_key, w_value, w_out)
    latent_out = lax.map(per_block, (tokens, labels)).reshape(LAT, H, W, C)
    act_grad = (out_grad.astype(jnp.float32) * slope_of(pre)).astype(jnp.bfloat16)
    grad_pad = jnp.pad(act_grad, ((0, 2), (1, 1), (1, 1), (0, 0)))
    flipped = jnp.swapaxes(jnp.flip(conv_weight, (0, 1, 2)), 3, 4)
    frame_grad = (out_grad.astype(jnp.float32) + conv_block(grad_pad, flipped)).astype(jnp.bfloat16)
    return (latent_out, frame_grad)
```

```python
import functools
import math

import jax
import jax.numpy as jnp
from jax import lax
from jax.experimental import pallas as pl
from jax.experimental.pallas import tpu as pltpu
from jax.sharding import PartitionSpec as P

HEAD = 64
KT, KH, KW = 3, 3, 3
DOWN = 8
LANES = 128
VMEM_MIB = 63
SPAN = 8
SLOT_DW = (1, 0, 2)
MESH = pl.DeviceIdType.MESH
F32, BF16 = jnp.float32, jnp.bfloat16


def dot(a, b):
    return jnp.dot(a, b, preferred_element_type=F32)


def dot_nt(a, b):
    return lax.dot_general(a, b, (((1,), (1,)), ((), ())), preferred_element_type=F32)


def kernel(
    n_tm, n_sc, reach,
    frames, conv_w, down_w, w_query, w_key, w_value, w_out, shots_hbm, labels_hbm, out_grad,
    latent_out, frame_grad,
    shots, labels, xin, gin, wb, wd, wqkv, wo, field, shift, taps, total, grouped, carry, mixes, kv, tokens, heads,
    edge_out, rim_out, edge_in, rim_in, corner_in, tail_out, tail_in,
    w_sem, load_sem, send_sem, recv_sem,
):
    T, R, W, C = xin.shape
    RC = R * C
    J = T // DOWN
    TW = T * W
    RIM = (KT - 1) * W
    M = TW + RIM
    NT = 256 if RC % 256 == 0 else C
    blocks = [slice(b, b + LANES) for b in range(0, RC, LANES)]
    i, s = lax.axis_index("tm"), lax.axis_index("scene")

    once = lax.div(i, jnp.int32(n_tm)) + 1
    loads = []

    def load(src, dst):
        copy = pltpu.make_async_copy(src, dst, load_sem.at[len(loads)])
        copy.start()
        loads.append(copy)
        return copy

    part = T // math.gcd(4, T)
    get_x = [load(frames.at[pl.ds(t, part)], xin.at[pl.ds(t, part)]) for t in range(0, T, part)]
    w_copies = [[[] for _ in range(R)] for _ in SLOT_DW]

    def load_weights(slot):
        for ho in range(R):
            for dt in range(KT):
                for hi in range(R):
                    copy = pltpu.make_async_copy(
                        conv_w.at[dt, hi - ho + 1, SLOT_DW[slot]],
                        wb.at[dt, pl.ds(slot * RC + hi * C, C), pl.ds(ho * C, C)],
                        w_sem.at[((slot * R + ho) * KT + dt) * R + hi],
                    )
                    copy.start()
                    w_copies[slot][ho].append(copy)

    load_weights(0)

    barrier = pltpu.get_barrier_semaphore()
    peers = []
    for d in range(1, reach + 1):
        peers += [(i + d < n_tm, (i + d, s)), (i - d >= 0, (i - d, s))]
    for o in range(1, n_sc):
        peers.append((None, (i, lax.rem(s + o, n_sc))))
    for a in (-1, 1):
        for b in (-1, 1):
            ok = (i + a >= 0) & (i + a < n_tm) & (s + b >= 0) & (s + b < n_sc)
            peers.append((ok, (i + a, s + b)))
    waits = jnp.int32(0)
    for ok, dev in peers:
        if ok is None:
            pl.semaphore_signal(barrier, inc=1, device_id=dev, device_id_type=MESH)
            waits = waits + 1
        else:
            @pl.when(ok)
            def _(dev=dev):
                pl.semaphore_signal(barrier, inc=1, device_id=dev, device_id_type=MESH)

            waits = waits + ok.astype(jnp.int32)
    pending = []

    def send(ok, src, dst, k, dev):
        copy = pltpu.make_async_remote_copy(
            src_ref=src, dst_ref=dst, send_sem=send_sem.at[k], recv_sem=recv_sem.at[k],
            device_id=dev, device_id_type=MESH,
        )
        pl.when(ok)(copy.start)
        pending.append((ok, copy))

    def receive(ok, dst, k, zero=True):
        copy = pltpu.make_async_remote_copy(
            src_ref=dst, dst_ref=dst, send_sem=send_sem.at[k], recv_sem=recv_sem.at[k],
            device_id=(i, s), device_id_type=MESH,
        )
        pl.when(ok)(copy.wait_recv)
        if zero:
            @pl.when(jnp.logical_not(ok))
            def _():
                dst[...] = jnp.zeros(dst.shape, dst.dtype)

    left_ok, right_ok = s > 0, s < n_sc - 1

    def send_halo(phase):
        base = W + (RIM if phase == 0 else 0)
        step = 1 if phase == 0 else -1
        rim_ok = (i < n_tm - 1) if phase == 0 else (i > 0)
        rim_row = base + TW - RIM if phase == 0 else base
        for b, lanes in enumerate(blocks):
            edge_out[phase, 0, :, lanes] = field[b, pl.ds(base + W - 1, T, stride=W), :].astype(BF16)
            edge_out[phase, 1, :, lanes] = field[b, pl.ds(base, T, stride=W), :].astype(BF16)
            rim_out[phase, :, lanes] = field[b, pl.ds(rim_row, RIM), :].astype(BF16)
        if phase == 0:
            pl.semaphore_wait(barrier, waits)
        k = phase * 5
        last = pl.ds(T - SPAN if phase == 0 else 0, SPAN)
        right_edge, left_edge = edge_out.at[phase, 0, last], edge_out.at[phase, 1, last]
        send(rim_ok & right_ok, right_edge, corner_in.at[phase, 0], k + 1, (i + step, s + 1))
        send(rim_ok & left_ok, left_edge, corner_in.at[phase, 1], k + 2, (i + step, s - 1))
        send(rim_ok, rim_out.at[phase], rim_in.at[phase], k, (i + step, s))
        send(right_ok, edge_out.at[phase, 0], edge_in.at[phase, 0], k + 3, (i, s + 1))
        send(left_ok, edge_out.at[phase, 1], edge_in.at[phase, 1], k + 4, (i, s - 1))

    def centre(phase):
        for b, lanes in enumerate(blocks):
            field[b, pl.ds(W if phase == 0 else W + TW, RIM), :] = jnp.zeros((RIM, LANES), F32)
            taps[:, lanes] = field[b, pl.ds(W, M), :].astype(BF16)

    def rim(phase):
        rim_ok = (i > 0) if phase == 0 else (i < n_tm - 1)
        receive(rim_ok, rim_in.at[phase], phase * 5)
        for b, lanes in enumerate(blocks):
            field[b, pl.ds(W if phase == 0 else W + TW, RIM), :] = rim_in[phase, :, lanes].astype(F32)
        own = rim_in[phase]
        at = 0 if phase == 0 else TW - RIM

        @pl.loop(0, RC // NT)
        def _(n):
            cols = pl.ds(pl.multiple_of(n * NT, NT), NT)
            part = total[at : at + RIM, cols]
            for dt in range(KT - 1):
                if phase == 0:
                    y = dot(own, wb[dt, 0:RC, cols])
                    y = y[dt * W :]
                    low, high = 0, dt * W
                else:
                    y = dot_nt(own, wb[dt, cols, :])
                    y = y[: RIM - dt * W]
                    low, high = dt * W, 0
                pads = [jnp.zeros((low, NT), F32)] * (low > 0) + [y] + [jnp.zeros((high, NT), F32)] * (high > 0)
                part = part + (jnp.concatenate(pads, axis=0) if len(pads) > 1 else y)
            total[at : at + RIM, cols] = part

    def sides(phase, wanted=(0, 1)):
        rim_ok = (i > 0) if phase == 0 else (i < n_tm - 1)
        k = phase * 5
        inner = RIM if phase == 0 else 0
        outer = 0 if phase == 0 else TW
        for side in wanted:
            ok = left_ok if side == 0 else right_ok
            receive(ok, edge_in.at[phase, side], k + 3 + side)
            receive(ok & rim_ok, corner_in.at[phase, side], k + 1 + side)
            at = 0 if side == 0 else W - 1
            near = SPAN - (KT - 1) if phase == 0 else 0
            slot = 1 + side if phase == 0 else 2 - side
            for b, lanes in enumerate(blocks):
                shift[b] = field[b, pl.ds(W - 1 if side == 0 else W + 1, M), :]
                shift[b, pl.ds(inner + at, T, stride=W), :] = edge_in[phase, side, :, lanes].astype(F32)
                corner = corner_in[phase, side, :, lanes].astype(F32)
                for t in range(KT - 1):
                    row = near + t
                    shift[b, pl.ds(outer + t * W + at, 1), :] = corner[row : row + 1, :]
                taps[:, slot * RC + lanes.start : slot * RC + lanes.stop] = shift[b].astype(BF16)

    def conv(phase, first, slots, add, tiles):
        lo, hi = first * RC, (first + slots) * RC
        def tile(n):
            cols = slice(n * NT, (n + 1) * NT)
            part = total[:, cols] if add else None
            for dt in range(KT):
                if phase == 0:
                    row = dt * W
                    ys = [dot(taps[row : row + TW, lo:hi], wb[dt, lo:hi, cols])]
                else:
                    row = (KT - 1 - dt) * W
                    ys = []
                    for at in range(lo, hi, RC):
                        rows = slice(at + cols.start, at + cols.stop)
                        ys.append(dot_nt(taps[row : row + TW, at : at + RC], wb[dt, rows, :]))
                for y in ys:
                    part = y if part is None else part + y
            total[:, cols] = part

        @pl.loop(0, once)
        def _(_):
            for n in tiles:
                tile(n)

    every = range(RC // NT)

    for copy in get_x:
        copy.wait()
    load_weights(1)
    load_weights(2)
    get_g = load(out_grad, gin)
    get_d = load(down_w, wd)
    get_qkv = [load(w, wqkv.at[:, pl.ds(k * C, C)]) for k, w in enumerate((w_query, w_key, w_value))]
    get_o = load(w_out, wo)
    get_index = [load(shots_hbm, shots), load(labels_hbm, labels)]
    for b, lanes in enumerate(blocks):
        field[b, 0:W, :] = jnp.zeros((W, LANES), F32)
        field[b, W + M :, :] = jnp.zeros((W, LANES), F32)
        h = lanes.start // C
        own = xin[:, h, :, lanes.start - h * C : lanes.stop - h * C]
        field[b, W + RIM : W + M, :] = own.astype(F32).reshape(TW, LANES)
    send_halo(0)
    centre(0)
    ready = 0
    for n in every:
        while ready * C < (n + 1) * NT:
            for copy in w_copies[0][ready]:
                copy.wait()
            ready += 1
        conv(0, 0, 1, False, (n,))
    rim(0)
    sides(0)
    for copies in w_copies[1] + w_copies[2]:
        for copy in copies:
            copy.wait()
    conv(0, 1, 2, True, every)

    get_g.wait()

    @pl.loop(0, J)
    def _(j):
        rows = pl.ds(pl.multiple_of(j * DOWN * W, DOWN * W), DOWN * W)
        span = pl.ds(pl.multiple_of(j * DOWN, DOWN), DOWN)
        for h in range(R):
            hc = slice(h * C, (h + 1) * C)
            pre = total[rows, hc]
            gate = jax.nn.sigmoid(pre)
            act = xin[span, h].astype(F32).reshape(DOWN * W, C) + pre * gate
            act = act.reshape(DOWN, W, C)
            for k in range(DOWN):
                grouped[pl.ds(pl.multiple_of((h * J + j) * W, W), W), k * C : (k + 1) * C] = act[k]
            slope = gate * (1.0 + pre * (1.0 - gate))
            grad = gin[span, h].astype(F32).reshape(DOWN * W, C) * slope
            for b, lanes in enumerate(blocks):
                if lanes.start // C == h:
                    own = grad[:, lanes.start - h * C : lanes.stop - h * C]
                    field[b, pl.ds(pl.multiple_of(W + j * DOWN * W, W), DOWN * W), :] = own

    send_halo(1)

    get_d.wait()

    @pl.loop(0, once)
    def _(_):
        kv[s] = dot(grouped[...].astype(BF16), wd[...].reshape(DOWN * C, C)).astype(BF16)

    for copy in get_index:
        copy.wait()
    starts, reached = [], jnp.int32(0)
    for k in range(shots.shape[0]):
        starts.append(reached)
        reached = reached + shots[k]

    def begin_of(t):
        best = jnp.int32(0)
        for start in starts:
            best = jnp.maximum(best, jnp.where(start <= t, start, 0))
        return best

    begins = [begin_of(i * J + j) for j in range(J)]

    def running_sums(latent):
        sums = [latent[:, 0]]
        for j in range(1, J):
            sums.append(latent[:, j] + sums[-1] * (begins[j] != i * J + j).astype(F32))
        return sums

    def latents(place):
        return kv[place].astype(F32).reshape(R, J, W, C)

    tail_out[...] = running_sums(latents(s))[-1]
    for d in range(1, reach + 1):
        send(i + d < n_tm, tail_out, tail_in.at[d - 1], 9 + d, (i + d, s))
    sibling = s + 1 - 2 * lax.rem(s, 2)
    far = range(1, n_sc // 2)
    hops = 1 + 2 * len(far)

    def spread(ref, k):
        send(True, ref.at[s], ref.at[s], k, (i, sibling))
        for o in far:
            send(True, ref.at[s], ref.at[s], k + o, (i, lax.rem(s + 2 * o, n_sc)))

    def relay(ref, k):
        for o in far:
            place = lax.rem(s + n_sc - 2 * o, n_sc)
            receive(s >= 0, ref.at[place], k + o, False)
            send(True, ref.at[place], ref.at[place], k + len(far) + o, (i, sibling))

    def arrive(ref, k):
        receive(s >= 0, ref.at[sibling], k, False)
        for o in far:
            place = lax.rem(sibling + n_sc - 2 * o, n_sc)
            receive(s >= 0, ref.at[place], k + len(far) + o, False)

    k_kv = 10 + reach
    k_carry = k_kv + hops
    spread(kv, k_kv)

    centre(1)
    conv(1, 0, 1, False, every)

    carried = jnp.zeros((R, W, C), F32)
    open_from = begin_of(i * J - 1)
    for d in range(1, reach + 1):
        receive(i - d >= 0, tail_in.at[d - 1], 9 + d)
        carried = carried + tail_in[d - 1] * (open_from <= (i - d) * J + J - 1).astype(F32)
    carry[s] = carried
    spread(carry, k_carry)

    rim(1)
    sides(1)
    conv(1, 1, 2, True, every[:1])
    relay(kv, k_kv)
    relay(carry, k_carry)
    conv(1, 1, 2, True, every[1:])

    @pl.loop(0, J)
    def _(j):
        rows = pl.ds(pl.multiple_of(j * DOWN * W, DOWN * W), DOWN * W)
        span = pl.ds(pl.multiple_of(j * DOWN, DOWN), DOWN)
        for h in range(R):
            grad = gin[span, h].astype(F32) + total[rows, h * C : (h + 1) * C].reshape(DOWN, W, C)
            frame_grad[span, h] = grad.astype(BF16)

    for copy in get_qkv + [get_o]:
        copy.wait()
    Q = R * J * W
    K = n_sc * Q

    def mix(place):
        latent, before = latents(place), carry[place]
        sums = running_sums(latent)
        for j in range(J):
            shot_sum = sums[j] + before * (begins[j] < i * J).astype(F32)
            whole = latent[:, j] + shot_sum / (i * J + j - begins[j] + 1).astype(F32)
            mixes[:, j] = whole
        tokens[place] = mixes[...].reshape(Q, C).astype(BF16)

    mix(s)
    mixed = tokens[s]
    query = dot(mixed, wqkv[:, 0:C]).astype(BF16)

    def frame_of(shape, dim):
        place = lax.broadcasted_iota(jnp.int32, shape, dim)
        return lax.rem(lax.div(place, jnp.int32(W)), jnp.int32(J))

    frame_q, frame_k = frame_of((Q, 1), 0), frame_of((1, K), 1)
    label_q, label_k = jnp.zeros((Q, 1), jnp.int32), jnp.zeros((1, K), jnp.int32)
    for j in range(J):
        label_q = jnp.where(frame_q == j, labels[j], label_q)
        label_k = jnp.where(frame_k == j, labels[j], label_k)
    allowed = (label_q == label_k) & (frame_k <= frame_q)
    arrive(kv, k_kv)
    arrive(carry, k_carry)
    for o in range(1, n_sc):
        mix(lax.rem(s + n_sc - o, n_sc))
    key_value = dot(tokens[...].reshape(K, C), wqkv[:, C:]).astype(BF16)
    per = 2
    lane = lax.broadcasted_iota(jnp.int32, (Q, per * HEAD), 1)
    for pair in range(C // (per * HEAD)):
        cols = slice(pair * per * HEAD, (pair + 1) * per * HEAD)
        q2, k2 = query[:, cols], key_value[:, cols]
        v2 = key_value[:, C + cols.start : C + cols.stop]
        out = None
        for one in range(per):
            mine = (lane >= one * HEAD) & (lane < (one + 1) * HEAD)
            q1 = jnp.where(mine, q2.astype(F32), 0.0).astype(BF16)
            scores = dot_nt(q1, k2) * (1.0 / math.sqrt(HEAD))
            scores = jnp.where(allowed, scores, -1000000000.0)
            expo = jnp.exp(scores - jnp.max(scores, axis=-1, keepdims=True))
            probs = (expo * (1.0 / jnp.sum(expo, axis=-1, keepdims=True))).astype(BF16)
            res = dot(probs, v2)
            out = res if out is None else jnp.where(mine, res, out)
        heads[:, cols] = out.astype(BF16)
    final = mixed.astype(F32) + dot(heads[...], wo[...])
    final = final.reshape(R, J, W, C)
    for h in range(R):
        latent_out[:, h] = final[h].astype(BF16)

    for ok, copy in pending:
        pl.when(ok)(copy.wait_send)


def passing(latent, grad, latent_to, grad_to, sem):
    puts = [pltpu.make_async_copy(grad, grad_to, sem.at[0]), pltpu.make_async_copy(latent, latent_to, sem.at[1])]
    for put in puts:
        put.start()
    for put in puts:
        put.wait()


def hand_over(latent, grad):
    latent, grad = (pltpu.with_memory_space_constraint(a, pltpu.VMEM) for a in (latent, grad))
    return pl.pallas_call(
        passing,
        out_shape=tuple(jax.ShapeDtypeStruct(a.shape, a.dtype) for a in (latent, grad)),
        in_specs=[pl.BlockSpec(memory_space=pltpu.VMEM)] * 2,
        out_specs=(pl.BlockSpec(memory_space=pltpu.HBM),) * 2,
        scratch_shapes=[pltpu.SemaphoreType.DMA((2,))],
    )(latent, grad)


def per_device(n_tm, n_sc, frames, conv_w, down_w, w_query, w_key, w_value, w_out, shots, labels, out_grad):
    T, R, W, C = frames.shape
    J = T // DOWN
    RC = R * C
    TW = T * W
    RIM = (KT - 1) * W
    M = TW + RIM
    reach = max(1, n_tm // 2)
    any_spec = pl.BlockSpec(memory_space=pltpu.HBM)
    vmem = pl.BlockSpec(memory_space=pltpu.VMEM)
    messages = 10 + reach + 2 * (n_sc - 1)
    results = pl.pallas_call(
        functools.partial(kernel, n_tm, n_sc, reach),
        out_shape=(
            pltpu.VMEM((J, R, W, C), BF16),
            pltpu.VMEM((T, R, W, C), BF16),
        ),
        in_specs=[any_spec] * 10,
        out_specs=(vmem, vmem),
        scratch_shapes=[
            pltpu.SMEM(shots.shape, jnp.int32),
            pltpu.SMEM((J,), jnp.int32),
            pltpu.VMEM((T, R, W, C), BF16),
            pltpu.VMEM((T, R, W, C), BF16),
            pltpu.VMEM((KT, KW * RC, RC), BF16),
            pltpu.VMEM((DOWN, C, C), BF16),
            pltpu.VMEM((C, 3 * C), BF16),
            pltpu.VMEM((C, C), BF16),
            pltpu.VMEM((RC // LANES, M + 2 * W, LANES), F32),
            pltpu.VMEM((RC // LANES, M, LANES), F32),
            pltpu.VMEM((M, KW * RC), BF16),
            pltpu.VMEM((TW, RC), F32),
            pltpu.VMEM((R * J * W, DOWN * C), F32),
            pltpu.VMEM((n_sc, R, W, C), F32),
            pltpu.VMEM((R, J, W, C), F32),
            pltpu.VMEM((n_sc, R * J * W, C), BF16),
            pltpu.VMEM((n_sc, R * J * W, C), BF16),
            pltpu.VMEM((R * J * W, C), BF16),
            pltpu.VMEM((2, 2, T, RC), BF16),
            pltpu.VMEM((2, RIM, RC), BF16),
            pltpu.VMEM((2, 2, T, RC), BF16),
            pltpu.VMEM((2, RIM, RC), BF16),
            pltpu.VMEM((2, 2, SPAN, RC), BF16),
            pltpu.VMEM((R, W, C), F32),
            pltpu.VMEM((reach, R, W, C), F32),
            pltpu.SemaphoreType.DMA((KT * KW * R * R,)),
            pltpu.SemaphoreType.DMA((13,)),
            pltpu.SemaphoreType.DMA((messages,)),
            pltpu.SemaphoreType.DMA((messages,)),
        ],
        compiler_params=pltpu.CompilerParams(
            collective_id=0, has_side_effects=True, vmem_limit_bytes=VMEM_MIB * 1024 * 1024
        ),
    )(frames, conv_w, down_w, w_query, w_key, w_value, w_out, shots, labels[:, 0], out_grad)
    return hand_over(*results)


def solution(mesh):
    in_specs = (
        P("tm", None, "scene", None), P(), P(), P(), P(), P(), P(), P(),
        P("tm", None), P("tm", None, "scene", None),
    )
    out_specs = (P("tm", None, "scene", None), P("tm", None, "scene", None))
    body = functools.partial(per_device, mesh.shape["tm"], mesh.shape["scene"])
    return jax.shard_map(body, mesh=mesh, in_specs=in_specs, out_specs=out_specs, check_vma=False)
```

```python
import functools
import math

import jax
import jax.numpy as jnp
from jax import lax
from jax.experimental import pallas as pl
from jax.experimental.pallas import tpu as pltpu
from jax.sharding import PartitionSpec as P

HEAD = 64
KT, KH, KW = 3, 3, 3
DOWN = 8
LANES = 128
VMEM_MIB = 63
SPAN = 8
SLOT_DW = (1, 0, 2)
MESH = pl.DeviceIdType.MESH
F32, BF16 = jnp.float32, jnp.bfloat16


def dot(a, b):
    return jnp.dot(a, b, preferred_element_type=F32)


def dot_nt(a, b):
    return lax.dot_general(a, b, (((1,), (1,)), ((), ())), preferred_element_type=F32)


def kernel(
    n_tm, n_sc, reach,
    frames, conv_w, down_w, w_query, w_key, w_value, w_out, shots_hbm, labels_hbm, out_grad,
    latent_out, frame_grad,
    shots, labels, xin, gin, wb, wd, wqkv, wo, field, shift, taps, total, grouped, carry, mixes, kv, tokens, heads,
    edge_out, rim_out, edge_in, rim_in, corner_in, tail_out, tail_in,
    w_sem, load_sem, send_sem, recv_sem,
):
    T, R, W, C = xin.shape
    RC = R * C
    J = T // DOWN
    TW = T * W
    RIM = (KT - 1) * W
    M = TW + RIM
    NT = 256 if RC % 256 == 0 else C
    blocks = [slice(b, b + LANES) for b in range(0, RC, LANES)]
    i, s = lax.axis_index("tm"), lax.axis_index("scene")

    once = lax.div(i, jnp.int32(n_tm)) + 1
    loads = []

    def load(src, dst):
        copy = pltpu.make_async_copy(src, dst, load_sem.at[len(loads)])
        copy.start()
        loads.append(copy)
        return copy

    part = T // math.gcd(4, T)
    get_x = [load(frames.at[pl.ds(t, part)], xin.at[pl.ds(t, part)]) for t in range(0, T, part)]
    w_copies = [[[] for _ in range(R)] for _ in SLOT_DW]

    def load_weights(slot):
        for ho in range(R):
            for dt in range(KT):
                for hi in range(R):
                    copy = pltpu.make_async_copy(
                        conv_w.at[dt, hi - ho + 1, SLOT_DW[slot]],
                        wb.at[dt, pl.ds(slot * RC + hi * C, C), pl.ds(ho * C, C)],
                        w_sem.at[((slot * R + ho) * KT + dt) * R + hi],
                    )
                    copy.start()
                    w_copies[slot][ho].append(copy)

    load_weights(0)

    barrier = pltpu.get_barrier_semaphore()
    peers = []
    for d in range(1, reach + 1):
        peers += [(i + d < n_tm, (i + d, s)), (i - d >= 0, (i - d, s))]
    for o in range(1, n_sc):
        peers.append((None, (i, lax.rem(s + o, n_sc))))
    for a in (-1, 1):
        for b in (-1, 1):
            ok = (i + a >= 0) & (i + a < n_tm) & (s + b >= 0) & (s + b < n_sc)
            peers.append((ok, (i + a, s + b)))
    waits = jnp.int32(0)
    for ok, dev in peers:
        if ok is None:
            pl.semaphore_signal(barrier, inc=1, device_id=dev, device_id_type=MESH)
            waits = waits + 1
        else:
            @pl.when(ok)
            def _(dev=dev):
                pl.semaphore_signal(barrier, inc=1, device_id=dev, device_id_type=MESH)

            waits = waits + ok.astype(jnp.int32)
    pending = []

    def send(ok, src, dst, k, dev):
        copy = pltpu.make_async_remote_copy(
            src_ref=src, dst_ref=dst, send_sem=send_sem.at[k], recv_sem=recv_sem.at[k],
            device_id=dev, device_id_type=MESH,
        )
        pl.when(ok)(copy.start)
        pending.append((ok, copy))

    def receive(ok, dst, k, zero=True):
        copy = pltpu.make_async_remote_copy(
            src_ref=dst, dst_ref=dst, send_sem=send_sem.at[k], recv_sem=recv_sem.at[k],
            device_id=(i, s), device_id_type=MESH,
        )
        pl.when(ok)(copy.wait_recv)
        if zero:
            @pl.when(jnp.logical_not(ok))
            def _():
                dst[...] = jnp.zeros(dst.shape, dst.dtype)

    left_ok, right_ok = s > 0, s < n_sc - 1

    def send_halo(phase):
        base = W + (RIM if phase == 0 else 0)
        step = 1 if phase == 0 else -1
        rim_ok = (i < n_tm - 1) if phase == 0 else (i > 0)
        rim_row = base + TW - RIM if phase == 0 else base
        for b, lanes in enumerate(blocks):
            edge_out[phase, 0, :, lanes] = field[b, pl.ds(base + W - 1, T, stride=W), :].astype(BF16)
            edge_out[phase, 1, :, lanes] = field[b, pl.ds(base, T, stride=W), :].astype(BF16)
            rim_out[phase, :, lanes] = field[b, pl.ds(rim_row, RIM), :].astype(BF16)
        if phase == 0:
            pl.semaphore_wait(barrier, waits)
        k = phase * 5
        last = pl.ds(T - SPAN if phase == 0 else 0, SPAN)
        right_edge, left_edge = edge_out.at[phase, 0, last], edge_out.at[phase, 1, last]
        send(rim_ok & right_ok, right_edge, corner_in.at[phase, 0], k + 1, (i + step, s + 1))
        send(rim_ok & left_ok, left_edge, corner_in.at[phase, 1], k + 2, (i + step, s - 1))
        send(rim_ok, rim_out.at[phase], rim_in.at[phase], k, (i + step, s))
        send(right_ok, edge_out.at[phase, 0], edge_in.at[phase, 0], k + 3, (i, s + 1))
        send(left_ok, edge_out.at[phase, 1], edge_in.at[phase, 1], k + 4, (i, s - 1))

    def centre(phase):
        for b, lanes in enumerate(blocks):
            field[b, pl.ds(W if phase == 0 else W + TW, RIM), :] = jnp.zeros((RIM, LANES), F32)
            taps[:, lanes] = field[b, pl.ds(W, M), :].astype(BF16)

    def rim(phase):
        rim_ok = (i > 0) if phase == 0 else (i < n_tm - 1)
        receive(rim_ok, rim_in.at[phase], phase * 5)
        for b, lanes in enumerate(blocks):
            field[b, pl.ds(W if phase == 0 else W + TW, RIM), :] = rim_in[phase, :, lanes].astype(F32)
        own = rim_in[phase]
        at = 0 if phase == 0 else TW - RIM

        @pl.loop(0, RC // NT)
        def _(n):
            cols = pl.ds(pl.multiple_of(n * NT, NT), NT)
            part = total[at : at + RIM, cols]
            for dt in range(KT - 1):
                if phase == 0:
                    y = dot(own, wb[dt, 0:RC, cols])
                    y = y[dt * W :]
                    low, high = 0, dt * W
                else:
                    y = dot_nt(own, wb[dt, cols, :])
                    y = y[: RIM - dt * W]
                    low, high = dt * W, 0
                pads = [jnp.zeros((low, NT), F32)] * (low > 0) + [y] + [jnp.zeros((high, NT), F32)] * (high > 0)
                part = part + (jnp.concatenate(pads, axis=0) if len(pads) > 1 else y)
            total[at : at + RIM, cols] = part

    def sides(phase, wanted=(0, 1)):
        rim_ok = (i > 0) if phase == 0 else (i < n_tm - 1)
        k = phase * 5
        inner = RIM if phase == 0 else 0
        outer = 0 if phase == 0 else TW
        for side in wanted:
            ok = left_ok if side == 0 else right_ok
            receive(ok, edge_in.at[phase, side], k + 3 + side)
            receive(ok & rim_ok, corner_in.at[phase, side], k + 1 + side)
            at = 0 if side == 0 else W - 1
            near = SPAN - (KT - 1) if phase == 0 else 0
            slot = 1 + side if phase == 0 else 2 - side
            for b, lanes in enumerate(blocks):
                shift[b] = field[b, pl.ds(W - 1 if side == 0 else W + 1, M), :]
                shift[b, pl.ds(inner + at, T, stride=W), :] = edge_in[phase, side, :, lanes].astype(F32)
                corner = corner_in[phase, side, :, lanes].astype(F32)
                for t in range(KT - 1):
                    row = near + t
                    shift[b, pl.ds(outer + t * W + at, 1), :] = corner[row : row + 1, :]
                taps[:, slot * RC + lanes.start : slot * RC + lanes.stop] = shift[b].astype(BF16)

    def conv(phase, first, slots, add, tiles):
        lo, hi = first * RC, (first + slots) * RC
        def tile(n):
            cols = slice(n * NT, (n + 1) * NT)
            part = total[:, cols] if add else None
            for dt in range(KT):
                if phase == 0:
                    row = dt * W
                    ys = [dot(taps[row : row + TW, lo:hi], wb[dt, lo:hi, cols])]
                else:
                    row = (KT - 1 - dt) * W
                    ys = []
                    for at in range(lo, hi, RC):
                        rows = slice(at + cols.start, at + cols.stop)
                        ys.append(dot_nt(taps[row : row + TW, at : at + RC], wb[dt, rows, :]))
                for y in ys:
                    part = y if part is None else part + y
            total[:, cols] = part

        @pl.loop(0, once)
        def _(_):
            for n in tiles:
                tile(n)

    every = range(RC // NT)

    for copy in get_x:
        copy.wait()
    load_weights(1)
    load_weights(2)
    get_g = load(out_grad, gin)
    get_d = load(down_w, wd)
    get_qkv = [load(w, wqkv.at[:, pl.ds(k * C, C)]) for k, w in enumerate((w_query, w_key, w_value))]
    get_o = load(w_out, wo)
    get_index = [load(shots_hbm, shots), load(labels_hbm, labels)]
    for b, lanes in enumerate(blocks):
        field[b, 0:W, :] = jnp.zeros((W, LANES), F32)
        field[b, W + M :, :] = jnp.zeros((W, LANES), F32)
        h = lanes.start // C
        own = xin[:, h, :, lanes.start - h * C : lanes.stop - h * C]
        field[b, W + RIM : W + M, :] = own.astype(F32).reshape(TW, LANES)
    send_halo(0)
    centre(0)
    ready = 0
    for n in every:
        while ready * C < (n + 1) * NT:
            for copy in w_copies[0][ready]:
                copy.wait()
            ready += 1
        conv(0, 0, 1, False, (n,))
    rim(0)
    sides(0)
    for copies in w_copies[1] + w_copies[2]:
        for copy in copies:
            copy.wait()
    conv(0, 1, 2, True, every)

    get_g.wait()

    @pl.loop(0, J)
    def _(j):
        rows = pl.ds(pl.multiple_of(j * DOWN * W, DOWN * W), DOWN * W)
        span = pl.ds(pl.multiple_of(j * DOWN, DOWN), DOWN)
        for h in range(R):
            hc = slice(h * C, (h + 1) * C)
            pre = total[rows, hc]
            gate = jax.nn.sigmoid(pre)
            act = xin[span, h].astype(F32).reshape(DOWN * W, C) + pre * gate
            act = act.reshape(DOWN, W, C)
            for k in range(DOWN):
                grouped[pl.ds(pl.multiple_of((h * J + j) * W, W), W), k * C : (k + 1) * C] = act[k]
            slope = gate * (1.0 + pre * (1.0 - gate))
            grad = gin[span, h].astype(F32).reshape(DOWN * W, C) * slope
            for b, lanes in enumerate(blocks):
                if lanes.start // C == h:
                    own = grad[:, lanes.start - h * C : lanes.stop - h * C]
                    field[b, pl.ds(pl.multiple_of(W + j * DOWN * W, W), DOWN * W), :] = own

    send_halo(1)

    get_d.wait()

    @pl.loop(0, once)
    def _(_):
        kv[s] = dot(grouped[...].astype(BF16), wd[...].reshape(DOWN * C, C)).astype(BF16)

    for copy in get_index:
        copy.wait()
    starts, reached = [], jnp.int32(0)
    for k in range(shots.shape[0]):
        starts.append(reached)
        reached = reached + shots[k]

    def begin_of(t):
        best = jnp.int32(0)
        for start in starts:
            best = jnp.maximum(best, jnp.where(start <= t, start, 0))
        return best

    begins = [begin_of(i * J + j) for j in range(J)]

    def running_sums(latent):
        sums = [latent[:, 0]]
        for j in range(1, J):
            sums.append(latent[:, j] + sums[-1] * (begins[j] != i * J + j).astype(F32))
        return sums

    def latents(place):
        return kv[place].astype(F32).reshape(R, J, W, C)

    tail_out[...] = running_sums(latents(s))[-1]
    for d in range(1, reach + 1):
        send(i + d < n_tm, tail_out, tail_in.at[d - 1], 9 + d, (i + d, s))
    sibling = s + 1 - 2 * lax.rem(s, 2)
    far = range(1, n_sc // 2)
    hops = 1 + 2 * len(far)

    def spread(ref, k):
        send(True, ref.at[s], ref.at[s], k, (i, sibling))
        for o in far:
            send(True, ref.at[s], ref.at[s], k + o, (i, lax.rem(s + 2 * o, n_sc)))

    def relay(ref, k):
        for o in far:
            place = lax.rem(s + n_sc - 2 * o, n_sc)
            receive(s >= 0, ref.at[place], k + o, False)
            send(True, ref.at[place], ref.at[place], k + len(far) + o, (i, sibling))

    def arrive(ref, k):
        receive(s >= 0, ref.at[sibling], k, False)
        for o in far:
            place = lax.rem(sibling + n_sc - 2 * o, n_sc)
            receive(s >= 0, ref.at[place], k + len(far) + o, False)

    k_kv = 10 + reach
    k_carry = k_kv + hops
    spread(kv, k_kv)

    centre(1)
    conv(1, 0, 1, False, every)

    rim(1)
    sides(1)
    conv(1, 1, 2, True, every[:1])
    relay(kv, k_kv)

    carried = jnp.zeros((R, W, C), F32)
    open_from = begin_of(i * J - 1)
    for d in range(1, reach + 1):
        receive(i - d >= 0, tail_in.at[d - 1], 9 + d)
        carried = carried + tail_in[d - 1] * (open_from <= (i - d) * J + J - 1).astype(F32)
    carry[s] = carried
    for o in range(1, n_sc):
        send(True, carry.at[s], carry.at[s], k_carry - 1 + o, (i, lax.rem(s + o, n_sc)))

    conv(1, 1, 2, True, every[1:])

    @pl.loop(0, J)
    def _(j):
        rows = pl.ds(pl.multiple_of(j * DOWN * W, DOWN * W), DOWN * W)
        span = pl.ds(pl.multiple_of(j * DOWN, DOWN), DOWN)
        for h in range(R):
            grad = gin[span, h].astype(F32) + total[rows, h * C : (h + 1) * C].reshape(DOWN, W, C)
            frame_grad[span, h] = grad.astype(BF16)

    for copy in get_qkv + [get_o]:
        copy.wait()
    Q = R * J * W
    K = n_sc * Q

    def mix(place):
        latent, before = latents(place), carry[place]
        sums = running_sums(latent)
        for j in range(J):
            shot_sum = sums[j] + before * (begins[j] < i * J).astype(F32)
            whole = latent[:, j] + shot_sum / (i * J + j - begins[j] + 1).astype(F32)
            mixes[:, j] = whole
        tokens[place] = mixes[...].reshape(Q, C).astype(BF16)

    mix(s)
    mixed = tokens[s]
    query = dot(mixed, wqkv[:, 0:C]).astype(BF16)

    def frame_of(shape, dim):
        place = lax.broadcasted_iota(jnp.int32, shape, dim)
        return lax.rem(lax.div(place, jnp.int32(W)), jnp.int32(J))

    frame_q, frame_k = frame_of((Q, 1), 0), frame_of((1, K), 1)
    label_q, label_k = jnp.zeros((Q, 1), jnp.int32), jnp.zeros((1, K), jnp.int32)
    for j in range(J):
        label_q = jnp.where(frame_q == j, labels[j], label_q)
        label_k = jnp.where(frame_k == j, labels[j], label_k)
    allowed = (label_q == label_k) & (frame_k <= frame_q)
    arrive(kv, k_kv)
    for o in range(1, n_sc):
        place = lax.rem(s + n_sc - o, n_sc)
        receive(s >= 0, carry.at[place], k_carry - 1 + o, False)
        mix(place)
    key_value = dot(tokens[...].reshape(K, C), wqkv[:, C:]).astype(BF16)
    per = 2
    lane = lax.broadcasted_iota(jnp.int32, (Q, per * HEAD), 1)
    for pair in range(C // (per * HEAD)):
        cols = slice(pair * per * HEAD, (pair + 1) * per * HEAD)
        q2, k2 = query[:, cols].astype(F32) * (1.0 / math.sqrt(HEAD)), key_value[:, cols]
        v2 = key_value[:, C + cols.start : C + cols.stop]
        mine = [(lane >= one * HEAD) & (lane < (one + 1) * HEAD) for one in range(per)]
        q1 = jnp.concatenate([jnp.where(m, q2, 0.0) for m in mine], axis=0).astype(BF16)
        scores = jnp.where(allowed[None], dot_nt(q1, k2).reshape(per, Q, K), -1000000000.0)
        expo = jnp.exp(scores - jnp.max(scores, axis=-1, keepdims=True))
        scale = 1.0 / jnp.sum(expo, axis=-1, keepdims=True)
        res = dot(expo.astype(BF16).reshape(per * Q, K), v2).reshape(per, Q, per * HEAD) * scale
        out = res[0]
        for one in range(1, per):
            out = jnp.where(mine[one], res[one], out)
        heads[:, cols] = out.astype(BF16)
    final = mixed.astype(F32) + dot(heads[...], wo[...])
    final = final.reshape(R, J, W, C)
    for h in range(R):
        latent_out[:, h] = final[h].astype(BF16)

    for ok, copy in pending:
        pl.when(ok)(copy.wait_send)


def passing(latent, grad, latent_to, grad_to, sem):
    puts = [pltpu.make_async_copy(grad, grad_to, sem.at[0]), pltpu.make_async_copy(latent, latent_to, sem.at[1])]
    for put in puts:
        put.start()
    for put in puts:
        put.wait()


def hand_over(latent, grad):
    latent, grad = (pltpu.with_memory_space_constraint(a, pltpu.VMEM) for a in (latent, grad))
    return pl.pallas_call(
        passing,
        out_shape=tuple(jax.ShapeDtypeStruct(a.shape, a.dtype) for a in (latent, grad)),
        in_specs=[pl.BlockSpec(memory_space=pltpu.VMEM)] * 2,
        out_specs=(pl.BlockSpec(memory_space=pltpu.HBM),) * 2,
        scratch_shapes=[pltpu.SemaphoreType.DMA((2,))],
    )(latent, grad)


def per_device(n_tm, n_sc, frames, conv_w, down_w, w_query, w_key, w_value, w_out, shots, labels, out_grad):
    T, R, W, C = frames.shape
    J = T // DOWN
    RC = R * C
    TW = T * W
    RIM = (KT - 1) * W
    M = TW + RIM
    reach = max(1, n_tm // 2)
    any_spec = pl.BlockSpec(memory_space=pltpu.HBM)
    vmem = pl.BlockSpec(memory_space=pltpu.VMEM)
    messages = 10 + reach + 2 * (n_sc - 1)
    results = pl.pallas_call(
        functools.partial(kernel, n_tm, n_sc, reach),
        out_shape=(
            pltpu.VMEM((J, R, W, C), BF16),
            pltpu.VMEM((T, R, W, C), BF16),
        ),
        in_specs=[any_spec] * 10,
        out_specs=(vmem, vmem),
        scratch_shapes=[
            pltpu.SMEM(shots.shape, jnp.int32),
            pltpu.SMEM((J,), jnp.int32),
            pltpu.VMEM((T, R, W, C), BF16),
            pltpu.VMEM((T, R, W, C), BF16),
            pltpu.VMEM((KT, KW * RC, RC), BF16),
            pltpu.VMEM((DOWN, C, C), BF16),
            pltpu.VMEM((C, 3 * C), BF16),
            pltpu.VMEM((C, C), BF16),
            pltpu.VMEM((RC // LANES, M + 2 * W, LANES), F32),
            pltpu.VMEM((RC // LANES, M, LANES), F32),
            pltpu.VMEM((M, KW * RC), BF16),
            pltpu.VMEM((TW, RC), F32),
            pltpu.VMEM((R * J * W, DOWN * C), F32),
            pltpu.VMEM((n_sc, R, W, C), F32),
            pltpu.VMEM((R, J, W, C), F32),
            pltpu.VMEM((n_sc, R * J * W, C), BF16),
            pltpu.VMEM((n_sc, R * J * W, C), BF16),
            pltpu.VMEM((R * J * W, C), BF16),
            pltpu.VMEM((2, 2, T, RC), BF16),
            pltpu.VMEM((2, RIM, RC), BF16),
            pltpu.VMEM((2, 2, T, RC), BF16),
            pltpu.VMEM((2, RIM, RC), BF16),
            pltpu.VMEM((2, 2, SPAN, RC), BF16),
            pltpu.VMEM((R, W, C), F32),
            pltpu.VMEM((reach, R, W, C), F32),
            pltpu.SemaphoreType.DMA((KT * KW * R * R,)),
            pltpu.SemaphoreType.DMA((13,)),
            pltpu.SemaphoreType.DMA((messages,)),
            pltpu.SemaphoreType.DMA((messages,)),
        ],
        compiler_params=pltpu.CompilerParams(
            collective_id=0, has_side_effects=True, vmem_limit_bytes=VMEM_MIB * 1024 * 1024
        ),
    )(frames, conv_w, down_w, w_query, w_key, w_value, w_out, shots, labels[:, 0], out_grad)
    return hand_over(*results)


def solution(mesh):
    in_specs = (
        P("tm", None, "scene", None), P(), P(), P(), P(), P(), P(), P(),
        P("tm", None), P("tm", None, "scene", None),
    )
    out_specs = (P("tm", None, "scene", None), P("tm", None, "scene", None))
    body = functools.partial(per_device, mesh.shape["tm"], mesh.shape["scene"])
    return jax.shard_map(body, mesh=mesh, in_specs=in_specs, out_specs=out_specs, check_vma=False)
```

```python
import functools
import math

import jax
import jax.numpy as jnp
from jax import lax
from jax.experimental import pallas as pl
from jax.experimental.pallas import tpu as pltpu
from jax.sharding import PartitionSpec as P

HEAD = 64
KT, KH, KW = 3, 3, 3
DOWN = 8
LANES = 128
VMEM_MIB = 63
SPAN = 8
SLOT_DW = (1, 0, 2)
MESH = pl.DeviceIdType.MESH
F32, BF16 = jnp.float32, jnp.bfloat16


def dot(a, b):
    return jnp.dot(a, b, preferred_element_type=F32)


def dot_nt(a, b):
    return lax.dot_general(a, b, (((1,), (1,)), ((), ())), preferred_element_type=F32)


def kernel(
    n_tm, n_sc, reach,
    frames, conv_w, down_w, w_query, w_key, w_value, w_out, shots_hbm, labels_hbm, out_grad,
    latent_out, frame_grad,
    shots, labels, xin, gin, wb, wd, wqkv, wo, field, shift, taps, total, grouped, carry, mixes, kv, tokens, heads,
    edge_out, rim_out, edge_in, rim_in, corner_in, tail_out, tail_in,
    w_sem, load_sem, send_sem, recv_sem,
):
    T, R, W, C = xin.shape
    RC = R * C
    J = T // DOWN
    TW = T * W
    RIM = (KT - 1) * W
    M = TW + RIM
    NT = 256 if RC % 256 == 0 else C
    blocks = [slice(b, b + LANES) for b in range(0, RC, LANES)]
    i, s = lax.axis_index("tm"), lax.axis_index("scene")

    once = lax.div(i, jnp.int32(n_tm)) + 1
    loads = []

    def load(src, dst):
        copy = pltpu.make_async_copy(src, dst, load_sem.at[len(loads)])
        copy.start()
        loads.append(copy)
        return copy

    part = T // math.gcd(4, T)
    get_x = [load(frames.at[pl.ds(t, part)], xin.at[pl.ds(t, part)]) for t in range(0, T, part)]
    w_copies = [[[] for _ in range(R)] for _ in SLOT_DW]

    def load_weights(slot):
        for ho in range(R):
            for dt in range(KT):
                for hi in range(R):
                    copy = pltpu.make_async_copy(
                        conv_w.at[dt, hi - ho + 1, SLOT_DW[slot]],
                        wb.at[dt, pl.ds(slot * RC + hi * C, C), pl.ds(ho * C, C)],
                        w_sem.at[((slot * R + ho) * KT + dt) * R + hi],
                    )
                    copy.start()
                    w_copies[slot][ho].append(copy)

    load_weights(0)

    barrier = pltpu.get_barrier_semaphore()
    peers = []
    for d in range(1, reach + 1):
        peers += [(i + d < n_tm, (i + d, s)), (i - d >= 0, (i - d, s))]
    for o in range(1, n_sc):
        peers.append((None, (i, lax.rem(s + o, n_sc))))
    for a in (-1, 1):
        for b in (-1, 1):
            ok = (i + a >= 0) & (i + a < n_tm) & (s + b >= 0) & (s + b < n_sc)
            peers.append((ok, (i + a, s + b)))
    waits = jnp.int32(0)
    for ok, dev in peers:
        if ok is None:
            pl.semaphore_signal(barrier, inc=1, device_id=dev, device_id_type=MESH)
            waits = waits + 1
        else:
            @pl.when(ok)
            def _(dev=dev):
                pl.semaphore_signal(barrier, inc=1, device_id=dev, device_id_type=MESH)

            waits = waits + ok.astype(jnp.int32)
    pending = []

    def send(ok, src, dst, k, dev):
        copy = pltpu.make_async_remote_copy(
            src_ref=src, dst_ref=dst, send_sem=send_sem.at[k], recv_sem=recv_sem.at[k],
            device_id=dev, device_id_type=MESH,
        )
        pl.when(ok)(copy.start)
        pending.append((ok, copy))

    def receive(ok, dst, k, zero=True):
        copy = pltpu.make_async_remote_copy(
            src_ref=dst, dst_ref=dst, send_sem=send_sem.at[k], recv_sem=recv_sem.at[k],
            device_id=(i, s), device_id_type=MESH,
        )
        pl.when(ok)(copy.wait_recv)
        if zero:
            @pl.when(jnp.logical_not(ok))
            def _():
                dst[...] = jnp.zeros(dst.shape, dst.dtype)

    left_ok, right_ok = s > 0, s < n_sc - 1

    def send_halo(phase):
        base = W + (RIM if phase == 0 else 0)
        step = 1 if phase == 0 else -1
        rim_ok = (i < n_tm - 1) if phase == 0 else (i > 0)
        rim_row = base + TW - RIM if phase == 0 else base
        for b, lanes in enumerate(blocks):
            edge_out[phase, 0, :, lanes] = field[b, pl.ds(base + W - 1, T, stride=W), :].astype(BF16)
            edge_out[phase, 1, :, lanes] = field[b, pl.ds(base, T, stride=W), :].astype(BF16)
            rim_out[phase, :, lanes] = field[b, pl.ds(rim_row, RIM), :].astype(BF16)
        if phase == 0:
            pl.semaphore_wait(barrier, waits)
        k = phase * 5
        last = pl.ds(T - SPAN if phase == 0 else 0, SPAN)
        right_edge, left_edge = edge_out.at[phase, 0, last], edge_out.at[phase, 1, last]
        send(rim_ok, rim_out.at[phase], rim_in.at[phase], k, (i + step, s))
        send(rim_ok & right_ok, right_edge, corner_in.at[phase, 0], k + 1, (i + step, s + 1))
        send(rim_ok & left_ok, left_edge, corner_in.at[phase, 1], k + 2, (i + step, s - 1))
        send(right_ok, edge_out.at[phase, 0], edge_in.at[phase, 0], k + 3, (i, s + 1))
        send(left_ok, edge_out.at[phase, 1], edge_in.at[phase, 1], k + 4, (i, s - 1))

    def centre(phase):
        for b, lanes in enumerate(blocks):
            field[b, pl.ds(W if phase == 0 else W + TW, RIM), :] = jnp.zeros((RIM, LANES), F32)
            taps[:, lanes] = field[b, pl.ds(W, M), :].astype(BF16)

    def rim(phase):
        rim_ok = (i > 0) if phase == 0 else (i < n_tm - 1)
        receive(rim_ok, rim_in.at[phase], phase * 5)
        for b, lanes in enumerate(blocks):
            field[b, pl.ds(W if phase == 0 else W + TW, RIM), :] = rim_in[phase, :, lanes].astype(F32)

    def shift_rows(phase, side, row, rows):
        for b in range(len(blocks)):
            shift[side, b, pl.ds(row, rows), :] = field[b, pl.ds((W - 1 if side == 0 else W + 1) + row, rows), :]

    def shift_own(phase):
        for side in (0, 1):
            shift_rows(phase, side, RIM if phase == 0 else 0, TW)

    def sides(phase, wanted=(0, 1)):
        rim_ok = (i > 0) if phase == 0 else (i < n_tm - 1)
        k = phase * 5
        inner = RIM if phase == 0 else 0
        outer = 0 if phase == 0 else TW
        for side in wanted:
            ok = left_ok if side == 0 else right_ok
            receive(ok, edge_in.at[phase, side], k + 3 + side)
            receive(ok & rim_ok, corner_in.at[phase, side], k + 1 + side)
            at = 0 if side == 0 else W - 1
            near = SPAN - (KT - 1) if phase == 0 else 0
            slot = 1 + side if phase == 0 else 2 - side
            shift_rows(phase, side, outer, RIM)
            for b, lanes in enumerate(blocks):
                shift[side, b, pl.ds(inner + at, T, stride=W), :] = edge_in[phase, side, :, lanes].astype(F32)
                corner = corner_in[phase, side, :, lanes].astype(F32)
                for t in range(KT - 1):
                    row = near + t
                    shift[side, b, pl.ds(outer + t * W + at, 1), :] = corner[row : row + 1, :]
                taps[:, slot * RC + lanes.start : slot * RC + lanes.stop] = shift[side, b].astype(BF16)

    def conv(phase, first, slots, add, tiles):
        lo, hi = first * RC, (first + slots) * RC
        def tile(n):
            cols = slice(n * NT, (n + 1) * NT)
            part = total[:, cols] if add else None
            for dt in range(KT):
                if phase == 0:
                    row = dt * W
                    ys = [dot(taps[row : row + TW, lo:hi], wb[dt, lo:hi, cols])]
                else:
                    row = (KT - 1 - dt) * W
                    ys = []
                    for at in range(lo, hi, RC):
                        rows = slice(at + cols.start, at + cols.stop)
                        ys.append(dot_nt(taps[row : row + TW, at : at + RC], wb[dt, rows, :]))
                for y in ys:
                    part = y if part is None else part + y
            total[:, cols] = part
            if not add:
                return
            own = rim_in[phase]
            for dt in range(KT - 1):
                if phase == 0:
                    y = dot(own, wb[dt, 0:RC, cols])[dt * W :]
                    at = 0
                else:
                    y = dot_nt(own, wb[dt, cols, :])[: RIM - dt * W]
                    at = TW - RIM + dt * W
                total[at : at + RIM - dt * W, cols] = total[at : at + RIM - dt * W, cols] + y

        @pl.loop(0, once)
        def _(_):
            if not add and tiles[0] == 0:
                shift_own(phase)
            for n in tiles:
                tile(n)

    every = range(RC // NT)

    for copy in get_x:
        copy.wait()
    load_weights(1)
    load_weights(2)
    for b, lanes in enumerate(blocks):
        field[b, 0:W, :] = jnp.zeros((W, LANES), F32)
        field[b, W + M :, :] = jnp.zeros((W, LANES), F32)
        h = lanes.start // C
        own = xin[:, h, :, lanes.start - h * C : lanes.stop - h * C]
        field[b, W + RIM : W + M, :] = own.astype(F32).reshape(TW, LANES)
    send_halo(0)
    centre(0)
    ready = 0
    for n in every:
        while ready * C < (n + 1) * NT:
            for copy in w_copies[0][ready]:
                copy.wait()
            ready += 1
        conv(0, 0, 1, False, (n,))
    get_g = load(out_grad, gin)
    get_d = load(down_w, wd)
    get_qkv = [load(w, wqkv.at[:, pl.ds(k * C, C)]) for k, w in enumerate((w_query, w_key, w_value))]
    get_o = load(w_out, wo)
    get_index = [load(shots_hbm, shots), load(labels_hbm, labels)]
    rim(0)
    sides(0)
    for copies in w_copies[1] + w_copies[2]:
        for copy in copies:
            copy.wait()
    conv(0, 1, 2, True, every)

    get_g.wait()

    @pl.loop(0, J)
    def _(j):
        rows = pl.ds(pl.multiple_of(j * DOWN * W, DOWN * W), DOWN * W)
        span = pl.ds(pl.multiple_of(j * DOWN, DOWN), DOWN)
        for h in range(R):
            hc = slice(h * C, (h + 1) * C)
            pre = total[rows, hc]
            gate = jax.nn.sigmoid(pre)
            act = xin[span, h].astype(F32).reshape(DOWN * W, C) + pre * gate
            act = act.reshape(DOWN, W, C)
            for k in range(DOWN):
                grouped[pl.ds(pl.multiple_of((h * J + j) * W, W), W), k * C : (k + 1) * C] = act[k]
            slope = gate * (1.0 + pre * (1.0 - gate))
            grad = gin[span, h].astype(F32).reshape(DOWN * W, C) * slope
            for b, lanes in enumerate(blocks):
                if lanes.start // C == h:
                    own = grad[:, lanes.start - h * C : lanes.stop - h * C]
                    field[b, pl.ds(pl.multiple_of(W + j * DOWN * W, W), DOWN * W), :] = own

    send_halo(1)

    get_d.wait()

    @pl.loop(0, once)
    def _(_):
        kv[s] = dot(grouped[...].astype(BF16), wd[...].reshape(DOWN * C, C)).astype(BF16)

    for copy in get_index:
        copy.wait()
    starts, reached = [], jnp.int32(0)
    for k in range(shots.shape[0]):
        starts.append(reached)
        reached = reached + shots[k]

    def begin_of(t):
        best = jnp.int32(0)
        for start in starts:
            best = jnp.maximum(best, jnp.where(start <= t, start, 0))
        return best

    begins = [begin_of(i * J + j) for j in range(J)]

    def running_sums(latent):
        sums = [latent[:, 0]]
        for j in range(1, J):
            sums.append(latent[:, j] + sums[-1] * (begins[j] != i * J + j).astype(F32))
        return sums

    def latents(place):
        return kv[place].astype(F32).reshape(R, J, W, C)

    tail_out[...] = running_sums(latents(s))[-1]
    for d in range(1, reach + 1):
        send(i + d < n_tm, tail_out, tail_in.at[d - 1], 9 + d, (i + d, s))
    sibling = s + 1 - 2 * lax.rem(s, 2)
    far = range(1, n_sc // 2)
    hops = 1 + 2 * len(far)

    def relay(ref, k):
        for o in far:
            place = lax.rem(s + n_sc - 2 * o, n_sc)
            receive(s >= 0, ref.at[place], k + o, False)
            send(True, ref.at[place], ref.at[place], k + len(far) + o, (i, sibling))

    def arrive(ref, k):
        receive(s >= 0, ref.at[sibling], k, False)
        for o in far:
            place = lax.rem(sibling + n_sc - 2 * o, n_sc)
            receive(s >= 0, ref.at[place], k + len(far) + o, False)

    k_kv = 10 + reach
    k_carry = k_kv + hops
    send(True, kv.at[s], kv.at[s], k_kv, (i, sibling))

    centre(1)
    conv(1, 0, 1, False, every)
    for o in far:
        send(True, kv.at[s], kv.at[s], k_kv + o, (i, lax.rem(s + 2 * o, n_sc)))

    rim(1)
    sides(1)
    conv(1, 1, 2, True, every[:1])
    carried = jnp.zeros((R, W, C), F32)
    open_from = begin_of(i * J - 1)
    for d in range(1, reach + 1):
        receive(i - d >= 0, tail_in.at[d - 1], 9 + d)
        carried = carried + tail_in[d - 1] * (open_from <= (i - d) * J + J - 1).astype(F32)
    carry[s] = carried
    for o in range(1, n_sc):
        send(True, carry.at[s], carry.at[s], k_carry - 1 + o, (i, lax.rem(s + o, n_sc)))

    conv(1, 1, 2, True, every[1:2])
    relay(kv, k_kv)
    conv(1, 1, 2, True, every[2:])

    @pl.loop(0, J)
    def _(j):
        rows = pl.ds(pl.multiple_of(j * DOWN * W, DOWN * W), DOWN * W)
        span = pl.ds(pl.multiple_of(j * DOWN, DOWN), DOWN)
        for h in range(R):
            grad = gin[span, h].astype(F32) + total[rows, h * C : (h + 1) * C].reshape(DOWN, W, C)
            frame_grad[span, h] = grad.astype(BF16)

    for copy in get_qkv + [get_o]:
        copy.wait()
    Q = R * J * W
    K = n_sc * Q

    def mix(place):
        latent, before = latents(place), carry[place]
        sums = running_sums(latent)
        for j in range(J):
            shot_sum = sums[j] + before * (begins[j] < i * J).astype(F32)
            whole = latent[:, j] + shot_sum / (i * J + j - begins[j] + 1).astype(F32)
            mixes[:, j] = whole
        tokens[place] = mixes[...].reshape(Q, C).astype(BF16)

    mix(s)
    mixed = tokens[s]
    query = dot(mixed, wqkv[:, 0:C]).astype(BF16)

    def frame_of(shape, dim):
        place = lax.broadcasted_iota(jnp.int32, shape, dim)
        return lax.rem(lax.div(place, jnp.int32(W)), jnp.int32(J))

    frame_q, frame_k = frame_of((Q, 1), 0), frame_of((1, K), 1)
    label_q, label_k = jnp.zeros((Q, 1), jnp.int32), jnp.zeros((1, K), jnp.int32)
    for j in range(J):
        label_q = jnp.where(frame_q == j, labels[j], label_q)
        label_k = jnp.where(frame_k == j, labels[j], label_k)
    allowed = (label_q == label_k) & (frame_k <= frame_q)
    arrive(kv, k_kv)
    for o in range(1, n_sc):
        place = lax.rem(s + n_sc - o, n_sc)
        receive(s >= 0, carry.at[place], k_carry - 1 + o, False)
        mix(place)
    key_value = dot(tokens[...].reshape(K, C), wqkv[:, C:]).astype(BF16)
    per = 2
    lane = lax.broadcasted_iota(jnp.int32, (Q, per * HEAD), 1)
    for pair in range(C // (per * HEAD)):
        cols = slice(pair * per * HEAD, (pair + 1) * per * HEAD)
        q2, k2 = query[:, cols].astype(F32) * (1.0 / math.sqrt(HEAD)), key_value[:, cols]
        v2 = key_value[:, C + cols.start : C + cols.stop]
        mine = [(lane >= one * HEAD) & (lane < (one + 1) * HEAD) for one in range(per)]
        q1 = jnp.concatenate([jnp.where(m, q2, 0.0) for m in mine], axis=0).astype(BF16)
        scores = jnp.where(allowed[None], dot_nt(q1, k2).reshape(per, Q, K), -1000000000.0)
        expo = jnp.exp(scores - jnp.max(scores, axis=-1, keepdims=True))
        scale = 1.0 / jnp.sum(expo, axis=-1, keepdims=True)
        res = dot(expo.astype(BF16).reshape(per * Q, K), v2).reshape(per, Q, per * HEAD) * scale
        out = res[0]
        for one in range(1, per):
            out = jnp.where(mine[one], res[one], out)
        heads[:, cols] = out.astype(BF16)
    final = mixed.astype(F32) + dot(heads[...], wo[...])
    final = final.reshape(R, J, W, C)
    for h in range(R):
        latent_out[:, h] = final[h].astype(BF16)

    for ok, copy in pending:
        pl.when(ok)(copy.wait_send)


def passing(latent, grad, latent_to, grad_to, sem):
    puts = [pltpu.make_async_copy(grad, grad_to, sem.at[0]), pltpu.make_async_copy(latent, latent_to, sem.at[1])]
    for put in puts:
        put.start()
    for put in puts:
        put.wait()


def hand_over(latent, grad):
    latent, grad = (pltpu.with_memory_space_constraint(a, pltpu.VMEM) for a in (latent, grad))
    return pl.pallas_call(
        passing,
        out_shape=tuple(jax.ShapeDtypeStruct(a.shape, a.dtype) for a in (latent, grad)),
        in_specs=[pl.BlockSpec(memory_space=pltpu.VMEM)] * 2,
        out_specs=(pl.BlockSpec(memory_space=pltpu.HBM),) * 2,
        scratch_shapes=[pltpu.SemaphoreType.DMA((2,))],
    )(latent, grad)


def per_device(n_tm, n_sc, frames, conv_w, down_w, w_query, w_key, w_value, w_out, shots, labels, out_grad):
    T, R, W, C = frames.shape
    J = T // DOWN
    RC = R * C
    TW = T * W
    RIM = (KT - 1) * W
    M = TW + RIM
    reach = max(1, n_tm // 2)
    any_spec = pl.BlockSpec(memory_space=pltpu.HBM)
    vmem = pl.BlockSpec(memory_space=pltpu.VMEM)
    messages = 10 + reach + 2 * (n_sc - 1)
    results = pl.pallas_call(
        functools.partial(kernel, n_tm, n_sc, reach),
        out_shape=(
            pltpu.VMEM((J, R, W, C), BF16),
            pltpu.VMEM((T, R, W, C), BF16),
        ),
        in_specs=[any_spec] * 10,
        out_specs=(vmem, vmem),
        scratch_shapes=[
            pltpu.SMEM(shots.shape, jnp.int32),
            pltpu.SMEM((J,), jnp.int32),
            pltpu.VMEM((T, R, W, C), BF16),
            pltpu.VMEM((T, R, W, C), BF16),
            pltpu.VMEM((KT, KW * RC, RC), BF16),
            pltpu.VMEM((DOWN, C, C), BF16),
            pltpu.VMEM((C, 3 * C), BF16),
            pltpu.VMEM((C, C), BF16),
            pltpu.VMEM((RC // LANES, M + 2 * W, LANES), F32),
            pltpu.VMEM((2, RC // LANES, M, LANES), F32),
            pltpu.VMEM((M, KW * RC), BF16),
            pltpu.VMEM((TW, RC), F32),
            pltpu.VMEM((R * J * W, DOWN * C), F32),
            pltpu.VMEM((n_sc, R, W, C), F32),
            pltpu.VMEM((R, J, W, C), F32),
            pltpu.VMEM((n_sc, R * J * W, C), BF16),
            pltpu.VMEM((n_sc, R * J * W, C), BF16),
            pltpu.VMEM((R * J * W, C), BF16),
            pltpu.VMEM((2, 2, T, RC), BF16),
            pltpu.VMEM((2, RIM, RC), BF16),
            pltpu.VMEM((2, 2, T, RC), BF16),
            pltpu.VMEM((2, RIM, RC), BF16),
            pltpu.VMEM((2, 2, SPAN, RC), BF16),
            pltpu.VMEM((R, W, C), F32),
            pltpu.VMEM((reach, R, W, C), F32),
            pltpu.SemaphoreType.DMA((KT * KW * R * R,)),
            pltpu.SemaphoreType.DMA((13,)),
            pltpu.SemaphoreType.DMA((messages,)),
            pltpu.SemaphoreType.DMA((messages,)),
        ],
        compiler_params=pltpu.CompilerParams(
            collective_id=0, has_side_effects=True, vmem_limit_bytes=VMEM_MIB * 1024 * 1024
        ),
    )(frames, conv_w, down_w, w_query, w_key, w_value, w_out, shots, labels[:, 0], out_grad)
    return hand_over(*results)


def solution(mesh):
    in_specs = (
        P("tm", None, "scene", None), P(), P(), P(), P(), P(), P(), P(),
        P("tm", None), P("tm", None, "scene", None),
    )
    out_specs = (P("tm", None, "scene", None), P("tm", None, "scene", None))
    body = functools.partial(per_device, mesh.shape["tm"], mesh.shape["scene"])
    return jax.shard_map(body, mesh=mesh, in_specs=in_specs, out_specs=out_specs, check_vma=False)
```

```python
import functools
import math

import jax
import jax.numpy as jnp
from jax import lax
from jax.experimental import pallas as pl
from jax.experimental.pallas import tpu as pltpu
from jax.sharding import PartitionSpec as P

HEAD = 64
KT, KH, KW = 3, 3, 3
DOWN = 8
LANES = 128
VMEM_MIB = 63
SPAN = 8
SLOT_DW = (1, 0, 2)
MESH = pl.DeviceIdType.MESH
F32, BF16 = jnp.float32, jnp.bfloat16


def dot(a, b):
    return jnp.dot(a, b, preferred_element_type=F32)


def dot_nt(a, b):
    return lax.dot_general(a, b, (((1,), (1,)), ((), ())), preferred_element_type=F32)


def kernel(
    n_tm, n_sc, reach,
    frames, conv_w, down_w, w_query, w_key, w_value, w_out, shots_hbm, labels_hbm, out_grad,
    latent_out, frame_grad,
    shots, labels, xin, gin, wb, wd, wqkv, wo, field, shift, taps, total, grouped, carry, mixes, kv, tokens, heads,
    edge_out, rim_out, edge_in, rim_in, corner_in, tail_out, tail_in,
    w_sem, load_sem, send_sem, recv_sem,
):
    T, R, W, C = xin.shape
    RC = R * C
    J = T // DOWN
    TW = T * W
    RIM = (KT - 1) * W
    M = TW + RIM
    NT = 256 if RC % 256 == 0 else C
    blocks = [slice(b, b + LANES) for b in range(0, RC, LANES)]
    i, s = lax.axis_index("tm"), lax.axis_index("scene")

    once = lax.div(i, jnp.int32(n_tm)) + 1
    loads = []

    def load(src, dst):
        copy = pltpu.make_async_copy(src, dst, load_sem.at[len(loads)])
        copy.start()
        loads.append(copy)
        return copy

    part = T // math.gcd(4, T)
    get_x = [load(frames.at[pl.ds(t, part)], xin.at[pl.ds(t, part)]) for t in range(0, T, part)]
    w_copies = [[[] for _ in range(R)] for _ in SLOT_DW]

    def load_weights(slot):
        for ho in range(R):
            for dt in range(KT):
                for hi in range(R):
                    copy = pltpu.make_async_copy(
                        conv_w.at[dt, hi - ho + 1, SLOT_DW[slot]],
                        wb.at[dt, pl.ds(slot * RC + hi * C, C), pl.ds(ho * C, C)],
                        w_sem.at[((slot * R + ho) * KT + dt) * R + hi],
                    )
                    copy.start()
                    w_copies[slot][ho].append(copy)

    load_weights(0)

    barrier = pltpu.get_barrier_semaphore()
    peers = []
    for d in range(1, reach + 1):
        peers += [(i + d < n_tm, (i + d, s)), (i - d >= 0, (i - d, s))]
    for o in range(1, n_sc):
        peers.append((None, (i, lax.rem(s + o, n_sc))))
    for a in (-1, 1):
        for b in (-1, 1):
            ok = (i + a >= 0) & (i + a < n_tm) & (s + b >= 0) & (s + b < n_sc)
            peers.append((ok, (i + a, s + b)))
    waits = jnp.int32(0)
    for ok, dev in peers:
        if ok is None:
            pl.semaphore_signal(barrier, inc=1, device_id=dev, device_id_type=MESH)
            waits = waits + 1
        else:
            @pl.when(ok)
            def _(dev=dev):
                pl.semaphore_signal(barrier, inc=1, device_id=dev, device_id_type=MESH)

            waits = waits + ok.astype(jnp.int32)
    pending = []

    def send(ok, src, dst, k, dev):
        copy = pltpu.make_async_remote_copy(
            src_ref=src, dst_ref=dst, send_sem=send_sem.at[k], recv_sem=recv_sem.at[k],
            device_id=dev, device_id_type=MESH,
        )
        pl.when(ok)(copy.start)
        pending.append((ok, copy))

    def receive(ok, dst, k, zero=True):
        copy = pltpu.make_async_remote_copy(
            src_ref=dst, dst_ref=dst, send_sem=send_sem.at[k], recv_sem=recv_sem.at[k],
            device_id=(i, s), device_id_type=MESH,
        )
        pl.when(ok)(copy.wait_recv)
        if zero:
            @pl.when(jnp.logical_not(ok))
            def _():
                dst[...] = jnp.zeros(dst.shape, dst.dtype)

    left_ok, right_ok = s > 0, s < n_sc - 1

    def send_halo(phase):
        base = W + (RIM if phase == 0 else 0)
        step = 1 if phase == 0 else -1
        rim_ok = (i < n_tm - 1) if phase == 0 else (i > 0)
        rim_row = base + TW - RIM if phase == 0 else base
        for b, lanes in enumerate(blocks):
            edge_out[phase, 0, :, lanes] = field[b, pl.ds(base + W - 1, T, stride=W), :].astype(BF16)
            edge_out[phase, 1, :, lanes] = field[b, pl.ds(base, T, stride=W), :].astype(BF16)
            rim_out[phase, :, lanes] = field[b, pl.ds(rim_row, RIM), :].astype(BF16)
        if phase == 0:
            pl.semaphore_wait(barrier, waits)
        k = phase * 5
        last = pl.ds(T - SPAN if phase == 0 else 0, SPAN)
        right_edge, left_edge = edge_out.at[phase, 0, last], edge_out.at[phase, 1, last]
        send(rim_ok, rim_out.at[phase], rim_in.at[phase], k, (i + step, s))
        send(rim_ok & right_ok, right_edge, corner_in.at[phase, 0], k + 1, (i + step, s + 1))
        send(rim_ok & left_ok, left_edge, corner_in.at[phase, 1], k + 2, (i + step, s - 1))
        send(right_ok, edge_out.at[phase, 0], edge_in.at[phase, 0], k + 3, (i, s + 1))
        send(left_ok, edge_out.at[phase, 1], edge_in.at[phase, 1], k + 4, (i, s - 1))

    def centre():
        for b, lanes in enumerate(blocks):
            field[b, W : W + RIM, :] = jnp.zeros((RIM, LANES), F32)
            taps[:, lanes] = field[b, pl.ds(W, M), :].astype(BF16)

    def rim(phase):
        rim_ok = (i > 0) if phase == 0 else (i < n_tm - 1)
        receive(rim_ok, rim_in.at[phase], phase * 5)
        for b, lanes in enumerate(blocks):
            field[b, pl.ds(W if phase == 0 else W + TW, RIM), :] = rim_in[phase, :, lanes].astype(F32)

    def shift_rows(phase, side, row, rows):
        for b in range(len(blocks)):
            shift[side, b, pl.ds(row, rows), :] = field[b, pl.ds((W - 1 if side == 0 else W + 1) + row, rows), :]

    def shift_own(phase):
        for side in (0, 1):
            shift_rows(phase, side, RIM if phase == 0 else 0, TW)

    def sides(phase, wanted=(0, 1)):
        rim_ok = (i > 0) if phase == 0 else (i < n_tm - 1)
        k = phase * 5
        inner = RIM if phase == 0 else 0
        outer = 0 if phase == 0 else TW
        for side in wanted:
            ok = left_ok if side == 0 else right_ok
            receive(ok, edge_in.at[phase, side], k + 3 + side)
            receive(ok & rim_ok, corner_in.at[phase, side], k + 1 + side)
            at = 0 if side == 0 else W - 1
            near = SPAN - (KT - 1) if phase == 0 else 0
            slot = 1 + side if phase == 0 else 2 - side
            shift_rows(phase, side, outer, RIM)
            for b, lanes in enumerate(blocks):
                shift[side, b, pl.ds(inner + at, T, stride=W), :] = edge_in[phase, side, :, lanes].astype(F32)
                corner = corner_in[phase, side, :, lanes].astype(F32)
                for t in range(KT - 1):
                    row = near + t
                    shift[side, b, pl.ds(outer + t * W + at, 1), :] = corner[row : row + 1, :]
                taps[:, slot * RC + lanes.start : slot * RC + lanes.stop] = shift[side, b].astype(BF16)

    def conv(phase, first, slots, add, tiles):
        lo, hi = first * RC, (first + slots) * RC
        def tile(n):
            cols = slice(n * NT, (n + 1) * NT)
            part = total[:, cols] if add else None
            for dt in range(KT):
                if phase == 0:
                    row = dt * W
                    ys = [dot(taps[row : row + TW, lo:hi], wb[dt, lo:hi, cols])]
                else:
                    row = (KT - 1 - dt) * W
                    ys = []
                    for at in range(lo, hi, RC):
                        rows = slice(at + cols.start, at + cols.stop)
                        ys.append(dot_nt(taps[row : row + TW, at : at + RC], wb[dt, rows, :]))
                for y in ys:
                    part = y if part is None else part + y
            total[:, cols] = part
            if not add:
                return
            own = rim_in[phase]
            for dt in range(KT - 1):
                if phase == 0:
                    y = dot(own, wb[dt, 0:RC, cols])[dt * W :]
                    at = 0
                else:
                    y = dot_nt(own, wb[dt, cols, :])[: RIM - dt * W]
                    at = TW - RIM + dt * W
                total[at : at + RIM - dt * W, cols] = total[at : at + RIM - dt * W, cols] + y
            if phase == 0:
                return
            for lanes in blocks:
                if cols.start <= lanes.start < cols.stop:
                    h = lanes.start // C
                    spot = slice(lanes.start - h * C, lanes.stop - h * C)
                    grad = gin[:, h, :, spot].astype(F32) + total[:, lanes].reshape(T, W, LANES)
                    frame_grad[:, h, :, spot] = grad.astype(BF16)

        @pl.loop(0, once)
        def _(_):
            if not add and tiles[0] == 0:
                shift_own(phase)
            for n in tiles:
                tile(n)

    every = range(RC // NT)

    for copy in get_x:
        copy.wait()
    load_weights(1)
    load_weights(2)
    for b, lanes in enumerate(blocks):
        field[b, 0:W, :] = jnp.zeros((W, LANES), F32)
        field[b, W + M :, :] = jnp.zeros((W, LANES), F32)
        h = lanes.start // C
        own = xin[:, h, :, lanes.start - h * C : lanes.stop - h * C]
        field[b, W + RIM : W + M, :] = own.astype(F32).reshape(TW, LANES)
    send_halo(0)
    centre()
    ready = 0
    for n in every:
        while ready * C < (n + 1) * NT:
            for copy in w_copies[0][ready]:
                copy.wait()
            ready += 1
        conv(0, 0, 1, False, (n,))
    get_g = load(out_grad, gin)
    get_d = load(down_w, wd)
    get_qkv = [load(w, wqkv.at[:, pl.ds(k * C, C)]) for k, w in enumerate((w_query, w_key, w_value))]
    get_o = load(w_out, wo)
    get_index = [load(shots_hbm, shots), load(labels_hbm, labels)]
    rim(0)
    sides(0)
    for copies in w_copies[1] + w_copies[2]:
        for copy in copies:
            copy.wait()
    conv(0, 1, 2, True, every)

    get_g.wait()

    @pl.loop(0, J)
    def _(j):
        rows = pl.ds(pl.multiple_of(j * DOWN * W, DOWN * W), DOWN * W)
        span = pl.ds(pl.multiple_of(j * DOWN, DOWN), DOWN)
        for h in range(R):
            hc = slice(h * C, (h + 1) * C)
            pre = total[rows, hc]
            gate = jax.nn.sigmoid(pre)
            act = xin[span, h].astype(F32).reshape(DOWN * W, C) + pre * gate
            act = act.reshape(DOWN, W, C)
            for k in range(DOWN):
                grouped[pl.ds(pl.multiple_of((h * J + j) * W, W), W), k * C : (k + 1) * C] = act[k]
            slope = gate * (1.0 + pre * (1.0 - gate))
            grad = gin[span, h].astype(F32).reshape(DOWN * W, C) * slope
            for b, lanes in enumerate(blocks):
                if lanes.start // C == h:
                    own = grad[:, lanes.start - h * C : lanes.stop - h * C]
                    field[b, pl.ds(pl.multiple_of(W + j * DOWN * W, W), DOWN * W), :] = own
                    taps[rows, lanes] = own.astype(BF16)

    send_halo(1)

    get_d.wait()

    @pl.loop(0, once)
    def _(_):
        kv[s] = dot(grouped[...].astype(BF16), wd[...].reshape(DOWN * C, C)).astype(BF16)

    for copy in get_index:
        copy.wait()
    starts, reached = [], jnp.int32(0)
    for k in range(shots.shape[0]):
        starts.append(reached)
        reached = reached + shots[k]

    def begin_of(t):
        best = jnp.int32(0)
        for start in starts:
            best = jnp.maximum(best, jnp.where(start <= t, start, 0))
        return best

    begins = [begin_of(i * J + j) for j in range(J)]

    def running_sums(latent):
        sums = [latent[:, 0]]
        for j in range(1, J):
            sums.append(latent[:, j] + sums[-1] * (begins[j] != i * J + j).astype(F32))
        return sums

    def latents(place):
        return kv[place].astype(F32).reshape(R, J, W, C)

    tail_out[...] = running_sums(latents(s))[-1]
    for d in range(1, reach + 1):
        send(i + d < n_tm, tail_out, tail_in.at[d - 1], 9 + d, (i + d, s))
    sibling = s + 1 - 2 * lax.rem(s, 2)
    far = range(1, n_sc // 2)
    hops = 1 + 2 * len(far)

    def relay(ref, k):
        for o in far:
            place = lax.rem(s + n_sc - 2 * o, n_sc)
            receive(s >= 0, ref.at[place], k + o, False)
            send(True, ref.at[place], ref.at[place], k + len(far) + o, (i, sibling))

    def arrive(ref, k):
        receive(s >= 0, ref.at[sibling], k, False)
        for o in far:
            place = lax.rem(sibling + n_sc - 2 * o, n_sc)
            receive(s >= 0, ref.at[place], k + len(far) + o, False)

    k_kv = 10 + reach
    k_carry = k_kv + hops
    send(True, kv.at[s], kv.at[s], k_kv, (i, sibling))

    taps[TW:, 0:RC] = jnp.zeros((RIM, RC), BF16)
    conv(1, 0, 1, False, every)
    for o in far:
        send(True, kv.at[s], kv.at[s], k_kv + o, (i, lax.rem(s + 2 * o, n_sc)))

    rim(1)
    sides(1)
    conv(1, 1, 2, True, every[:1])
    carried = jnp.zeros((R, W, C), F32)
    open_from = begin_of(i * J - 1)
    for d in range(1, reach + 1):
        receive(i - d >= 0, tail_in.at[d - 1], 9 + d)
        carried = carried + tail_in[d - 1] * (open_from <= (i - d) * J + J - 1).astype(F32)
    carry[s] = carried
    for o in range(1, n_sc):
        send(True, carry.at[s], carry.at[s], k_carry - 1 + o, (i, lax.rem(s + o, n_sc)))

    conv(1, 1, 2, True, every[1:2])
    relay(kv, k_kv)
    conv(1, 1, 2, True, every[2:])

    for copy in get_qkv + [get_o]:
        copy.wait()
    Q = R * J * W
    K = n_sc * Q

    def mix(place):
        latent, before = latents(place), carry[place]
        sums = running_sums(latent)
        for j in range(J):
            shot_sum = sums[j] + before * (begins[j] < i * J).astype(F32)
            whole = latent[:, j] + shot_sum / (i * J + j - begins[j] + 1).astype(F32)
            mixes[:, j] = whole
        tokens[place] = mixes[...].reshape(Q, C).astype(BF16)

    mix(s)
    arrive(kv, k_kv)
    for o in range(1, n_sc):
        place = lax.rem(s + n_sc - o, n_sc)
        receive(s >= 0, carry.at[place], k_carry - 1 + o, False)
        mix(place)

    @pl.loop(0, once)
    def _(_):
        mixed = tokens[s]
        query = dot(mixed, wqkv[:, 0:C]).astype(BF16)

        def frame_of(shape, dim):
            place = lax.broadcasted_iota(jnp.int32, shape, dim)
            return lax.rem(lax.div(place, jnp.int32(W)), jnp.int32(J))

        frame_q, frame_k = frame_of((Q, 1), 0), frame_of((1, K), 1)
        label_q, label_k = jnp.zeros((Q, 1), jnp.int32), jnp.zeros((1, K), jnp.int32)
        for j in range(J):
            label_q = jnp.where(frame_q == j, labels[j], label_q)
            label_k = jnp.where(frame_k == j, labels[j], label_k)
        allowed = (label_q == label_k) & (frame_k <= frame_q)
        key_value = dot(tokens[...].reshape(K, C), wqkv[:, C:]).astype(BF16)
        per = 2
        lane = lax.broadcasted_iota(jnp.int32, (Q, per * HEAD), 1)
        for pair in range(C // (per * HEAD)):
            cols = slice(pair * per * HEAD, (pair + 1) * per * HEAD)
            q2, k2 = query[:, cols].astype(F32) * (1.0 / math.sqrt(HEAD)), key_value[:, cols]
            v2 = key_value[:, C + cols.start : C + cols.stop]
            mine = [(lane >= one * HEAD) & (lane < (one + 1) * HEAD) for one in range(per)]
            q1 = jnp.concatenate([jnp.where(m, q2, 0.0) for m in mine], axis=0).astype(BF16)
            scores = jnp.where(allowed[None], dot_nt(q1, k2).reshape(per, Q, K), -1000000000.0)
            expo = jnp.exp(scores - jnp.max(scores, axis=-1, keepdims=True))
            scale = 1.0 / jnp.sum(expo, axis=-1, keepdims=True)
            res = dot(expo.astype(BF16).reshape(per * Q, K), v2).reshape(per, Q, per * HEAD) * scale
            out = res[0]
            for one in range(1, per):
                out = jnp.where(mine[one], res[one], out)
            heads[:, cols] = out.astype(BF16)
        final = mixed.astype(F32) + dot(heads[...], wo[...])
        final = final.reshape(R, J, W, C)
        for h in range(R):
            latent_out[:, h] = final[h].astype(BF16)

    for ok, copy in pending:
        pl.when(ok)(copy.wait_send)


def passing(latent, grad, latent_to, grad_to, sem):
    puts = [pltpu.make_async_copy(grad, grad_to, sem.at[0]), pltpu.make_async_copy(latent, latent_to, sem.at[1])]
    for put in puts:
        put.start()
    for put in puts:
        put.wait()


def hand_over(latent, grad):
    latent, grad = (pltpu.with_memory_space_constraint(a, pltpu.VMEM) for a in (latent, grad))
    return pl.pallas_call(
        passing,
        out_shape=tuple(jax.ShapeDtypeStruct(a.shape, a.dtype) for a in (latent, grad)),
        in_specs=[pl.BlockSpec(memory_space=pltpu.VMEM)] * 2,
        out_specs=(pl.BlockSpec(memory_space=pltpu.HBM),) * 2,
        scratch_shapes=[pltpu.SemaphoreType.DMA((2,))],
    )(latent, grad)


def per_device(n_tm, n_sc, frames, conv_w, down_w, w_query, w_key, w_value, w_out, shots, labels, out_grad):
    T, R, W, C = frames.shape
    J = T // DOWN
    RC = R * C
    TW = T * W
    RIM = (KT - 1) * W
    M = TW + RIM
    reach = max(1, n_tm // 2)
    any_spec = pl.BlockSpec(memory_space=pltpu.HBM)
    vmem = pl.BlockSpec(memory_space=pltpu.VMEM)
    messages = 10 + reach + 2 * (n_sc - 1)
    results = pl.pallas_call(
        functools.partial(kernel, n_tm, n_sc, reach),
        out_shape=(
            pltpu.VMEM((J, R, W, C), BF16),
            pltpu.VMEM((T, R, W, C), BF16),
        ),
        in_specs=[any_spec] * 10,
        out_specs=(vmem, vmem),
        scratch_shapes=[
            pltpu.SMEM(shots.shape, jnp.int32),
            pltpu.SMEM((J,), jnp.int32),
            pltpu.VMEM((T, R, W, C), BF16),
            pltpu.VMEM((T, R, W, C), BF16),
            pltpu.VMEM((KT, KW * RC, RC), BF16),
            pltpu.VMEM((DOWN, C, C), BF16),
            pltpu.VMEM((C, 3 * C), BF16),
            pltpu.VMEM((C, C), BF16),
            pltpu.VMEM((RC // LANES, M + 2 * W, LANES), F32),
            pltpu.VMEM((2, RC // LANES, M, LANES), F32),
            pltpu.VMEM((M, KW * RC), BF16),
            pltpu.VMEM((TW, RC), F32),
            pltpu.VMEM((R * J * W, DOWN * C), F32),
            pltpu.VMEM((n_sc, R, W, C), F32),
            pltpu.VMEM((R, J, W, C), F32),
            pltpu.VMEM((n_sc, R * J * W, C), BF16),
            pltpu.VMEM((n_sc, R * J * W, C), BF16),
            pltpu.VMEM((R * J * W, C), BF16),
            pltpu.VMEM((2, 2, T, RC), BF16),
            pltpu.VMEM((2, RIM, RC), BF16),
            pltpu.VMEM((2, 2, T, RC), BF16),
            pltpu.VMEM((2, RIM, RC), BF16),
            pltpu.VMEM((2, 2, SPAN, RC), BF16),
            pltpu.VMEM((R, W, C), F32),
            pltpu.VMEM((reach, R, W, C), F32),
            pltpu.SemaphoreType.DMA((KT * KW * R * R,)),
            pltpu.SemaphoreType.DMA((13,)),
            pltpu.SemaphoreType.DMA((messages,)),
            pltpu.SemaphoreType.DMA((messages,)),
        ],
        compiler_params=pltpu.CompilerParams(
            collective_id=0, has_side_effects=True, vmem_limit_bytes=VMEM_MIB * 1024 * 1024
        ),
    )(frames, conv_w, down_w, w_query, w_key, w_value, w_out, shots, labels[:, 0], out_grad)
    return hand_over(*results)


def solution(mesh):
    in_specs = (
        P("tm", None, "scene", None), P(), P(), P(), P(), P(), P(), P(),
        P("tm", None), P("tm", None, "scene", None),
    )
    out_specs = (P("tm", None, "scene", None), P("tm", None, "scene", None))
    body = functools.partial(per_device, mesh.shape["tm"], mesh.shape["scene"])
    return jax.shard_map(body, mesh=mesh, in_specs=in_specs, out_specs=out_specs, check_vma=False)
```
